32 devices in a mesh: lat: 4 (over y, x), lon: 8 (over z, core).
Axes of the slice: x: 2, y: 2, z: 4, core: 2. Of those that a mesh axis runs over, the one named last changes fastest.
Arguments:
- field: float32 [80, 160, 384], P('lat', 'lon'), may hold values from -6 to 6
- lat_kernel: float32 [41], replicated, may hold values from 0.0121951215 to 0.036585364
- lon_kernel: float32 [41], replicated, may hold values from 0.0121951215 to 0.036585364
- time_taps: float32 [129], replicated, may hold values from -0.0058139535 to 0.0058139535
Outputs:
- basis: float32 [80, 160, 256], P('lat', 'lon')
- merged_factor: float32 [256, 256], replicated
The draws below stay inside these ranges and needn't reach their ends.
All inputs are finite; a program needn't handle non-finite values.
Results may differ from the reference program's by a relative error of at most 0.00016.
Values sent between devices are 32-bit elements; how exact they have to be, the bound alone decides.
A program may use at most 64 MiB of HBM per device.

```python
import jax
import jax.numpy as jnp
from jax import lax

TH = 64
SH = 20
TIN = 384
NLAT = 80
NLON = 160


def block_levels(rng, shape, pieces, smallest, top_value):
    level = 1.0
    for axis_at, shards_of in pieces:
        steps = jax.random.uniform(jax.random.fold_in(jax.random.fold_in(rng, 6), axis_at), (shards_of,), jnp.float32, smallest / len(pieces), top_value / len(pieces))
        level = level * jnp.repeat(jnp.exp(steps), shape[axis_at] // shards_of).reshape((-1,) + (1,) * (len(shape) - 1 - axis_at))
    return level


def normal_values(own_key, shape, spread, limit, cuts=(), kind=jnp.bfloat16):
    result = jax.random.normal(own_key, shape, jnp.float32) * spread
    if len(cuts) > 0:
        result = block_levels(own_key, shape, cuts, -0.22, 0.18) * result
    return jnp.clip(result, min=-limit, max=limit).astype(kind)


def setup_inputs(seed: int = 0) -> dict:
    arg_keys = jax.random.split(jax.random.key(seed), 5)
    return {
        "field": normal_values(arg_keys[0], (NLAT, NLON, TIN), 1.0, 6.0, ((0, 4), (1, 8)), jnp.float32),
        "lat_kernel": jnp.clip(jax.random.uniform(arg_keys[1], (2 * SH + 1,), jnp.float32, 0.0121951215, 0.036585364), 0.0121951215, 0.036585364),
        "lon_kernel": jnp.clip(jax.random.uniform(arg_keys[2], (2 * SH + 1,), jnp.float32, 0.0121951215, 0.036585364), 0.0121951215, 0.036585364),
        "time_taps": jnp.clip(jax.random.uniform(arg_keys[3], (2 * TH + 1,), jnp.float32, -0.0058139535, 0.0058139535), -0.0058139535, 0.0058139535),
    }


def reference(field, lat_kernel, lon_kernel, time_taps):
    nrows, ncols, length_in = field.shape
    steps_out = length_in - 2 * TH
    source = lax.broadcasted_iota(jnp.int32, (length_in, steps_out), 0)
    target = lax.broadcasted_iota(jnp.int32, (length_in, steps_out), 1)
    offset = source - target
    inside = (offset >= 0) & (offset <= 2 * TH)
    toeplitz = jnp.where(inside, time_taps[jnp.clip(offset, 0, 2 * TH)], jnp.float32(0.0))
    toeplitz = toeplitz + jnp.where(offset == TH, jnp.float32(1.0), jnp.float32(0.0))
    filtered = jnp.dot(field.reshape(-1, length_in).astype(jnp.float32), toeplitz.astype(jnp.float32), precision=lax.Precision.HIGHEST, preferred_element_type=jnp.float32).reshape(nrows, ncols, steps_out)
    padded = jnp.pad(filtered, ((SH, SH), (0, 0), (0, 0)))
    lat_done = jnp.zeros_like(filtered)
    for shift_k in range(2 * SH + 1):
        lat_done = lat_done + lat_kernel[shift_k] * padded[shift_k:shift_k + nrows]
    wrapped = jnp.concatenate([lat_done[:, ncols - SH:], lat_done, lat_done[:, :SH]], axis=1)
    smooth = jnp.zeros_like(filtered)
    for shift_k in range(2 * SH + 1):
        smooth = smooth + lon_kernel[shift_k] * wrapped[:, shift_k:shift_k + ncols]
    latitude = jnp.pi * (jnp.arange(nrows, dtype=jnp.float32) + 0.5) / nrows - jnp.pi / 2
    weights = jnp.sqrt(jnp.cos(latitude))
    matrix = (smooth * weights[:, None, None]).reshape(-1, steps_out)
    gram = lax.dot_general(matrix.astype(jnp.float32), matrix.astype(jnp.float32), (((0,), (0,)), ((), ())), precision=lax.Precision.HIGHEST, preferred_element_type=jnp.float32)
    lower = jnp.linalg.cholesky(gram)
    scale = jnp.sqrt(jnp.float32(nrows * ncols))
    solved = lax.linalg.triangular_solve(lower, matrix, left_side=False, lower=True, transpose_a=True)
    basis = (solved * scale).reshape(nrows, ncols, steps_out)
    return (basis, lower.T / scale)
```

```python
import functools

import jax
import jax.numpy as jnp
import numpy as np
from jax import lax
from jax.experimental import pallas as pl
from jax.experimental.pallas import tpu as pltpu
from jax.sharding import PartitionSpec as P


MESH = pl.DeviceIdType.MESH
NB = 32
LANES = 128


def factor_kernel(scale, n, g_ref, m_ref, r_ref, basis_ref, a, b, y_ref):
    at = 0
    for t in range(0, n, LANES):
        if t:
            a[t:t + LANES, :t] = jnp.zeros((LANES, t), jnp.float32)
        for q in range(t, n, LANES):
            a[t:t + LANES, q:q + LANES] = g_ref[at:at + LANES]
            at += LANES
    b[...] = (lax.broadcasted_iota(jnp.int32, (n, n), 0) == lax.broadcasted_iota(jnp.int32, (n, n), 1)).astype(jnp.float32)
    sub = lax.broadcasted_iota(jnp.int32, (8, LANES), 0)
    tiles = n // LANES
    for k in range(0, n, NB):
        kt = k // LANES
        live = [(a, t) for t in range(kt, tiles)] + [(b, t) for t in range(kt + 1)]
        grp = [[ref[k + 8 * h:k + 8 * h + 8, t * LANES:(t + 1) * LANES] for ref, t in live] for h in range(NB // 8)]
        for g in range(NB // 8):
            hs = range(g, NB // 8)
            lane = k + 8 * g - kt * LANES
            cols = [{h: jnp.broadcast_to(grp[h][0][:, lane + q:lane + q + 1], (8, LANES)) for h in hs} for q in range(8)]
            done = None
            for q in range(8):
                d = jnp.broadcast_to(cols[q][g][q:q + 1, :], (8, LANES))
                inv = 1.0 / d
                u = {h: cols[q][h] * inv for h in hs}
                u[g] = jnp.where(sub > q, u[g], 0.0)
                for p in range(q + 1, 8):
                    e = jnp.broadcast_to(cols[p][g][q:q + 1, :], (8, LANES))
                    for h in hs:
                        cols[p][h] = cols[p][h] - u[h] * e
                root = lax.sqrt(d)
                done = root if done is None else jnp.where(sub == q, root, done)
                for t in range(len(live)):
                    row = jnp.broadcast_to(grp[g][t][q:q + 1, :], (8, LANES))
                    for h in hs:
                        grp[h][t] = grp[h][t] - u[h] * row
            rinv = 1.0 / done
            for t in range(len(live)):
                grp[g][t] = grp[g][t] * rinv
        panel = jnp.concatenate([jnp.concatenate(x, axis=1) for x in grp], axis=0)
        n_a = tiles - kt
        row_id = lax.broadcasted_iota(jnp.int32, (NB, n_a * LANES), 0) + k
        lane_id = lax.broadcasted_iota(jnp.int32, (NB, n_a * LANES), 1) + kt * LANES
        pa = panel[:, :n_a * LANES]
        pb = panel[:, n_a * LANES:]
        if kt:
            r_ref[k:k + NB, :kt * LANES] = jnp.zeros((NB, kt * LANES), jnp.float32)
        r_ref[k:k + NB, kt * LANES:] = jnp.where(lane_id >= row_id, pa / scale, 0.0)
        y_ref[k:k + NB, :(kt + 1) * LANES] = pb * scale
        if kt + 1 < tiles:
            y_ref[k:k + NB, (kt + 1) * LANES:] = jnp.zeros((NB, n - (kt + 1) * LANES), jnp.float32)
        nxt = k + NB
        if nxt < n:
            nt = nxt // LANES
            left = panel[:, (nt - kt) * LANES:n_a * LANES]
            dims = (((0,), (0,)), ((), ()))
            right = panel[:, (nt - kt) * LANES:]
            upd = lax.dot_general(left, right, dims, precision=lax.Precision.HIGHEST, preferred_element_type=jnp.float32)
            upd = upd[nxt - nt * LANES:]
            w_a = n - nt * LANES
            a[nxt:, nt * LANES:] = a[nxt:, nt * LANES:] - upd[:, :w_a]
            b[nxt:, :(kt + 1) * LANES] = b[nxt:, :(kt + 1) * LANES] - upd[:, w_a:]
        if nxt % LANES == 0:
            at = kt * LANES
            part = lax.dot_general(
                m_ref[:, :nxt], y_ref[at:nxt, :nxt], (((1,), (1,)), ((), ())),
                precision=lax.Precision.HIGHEST, preferred_element_type=jnp.float32)
            cols = basis_ref.shape[1]
            for i in range(basis_ref.shape[0]):
                basis_ref[i, :, at:nxt] = part[i * cols:(i + 1) * cols]


def factor(gram, matrix, scale, rows, cols):
    n = matrix.shape[1]
    square = jax.ShapeDtypeStruct((n, n), jnp.float32)
    vmem = pl.BlockSpec(memory_space=pltpu.VMEM)
    return pl.pallas_call(
        functools.partial(factor_kernel, scale, n),
        out_shape=(square, jax.ShapeDtypeStruct((rows, cols, n), jnp.float32)),
        in_specs=[vmem, vmem],
        out_specs=(vmem, vmem),
        scratch_shapes=[pltpu.VMEM((n, n), jnp.float32)] * 3,
        name="factor",
    )(gram, matrix)


def front_kernel(n_lat, n_lon, pair, cols, group, x_ref, v_ref, lat_ref, lon_ref, w_ref, m_ref, out_ref, flat, row_ref, band_ref, ext, lonb, g_ref, rbuf, zbuf, psend, precv, fsend, frecv, lsend, lrecv, ssem, rsem, zssem, zrsem, cssem, crsem):
    lat, lon = lax.axis_index("lat"), lax.axis_index("lon")
    n_p, n_z = n_lat * pair, n_lon // pair
    share = g_ref.shape[0] // n_p
    core, z = lax.rem(lon, pair), lon // pair
    me = lat * pair + core
    chunks, size = lonb.shape[0], lonb.shape[2]
    rows_lat = size // cols
    taps = lat_ref.shape[0]
    step = group * cols
    pieces = size // step
    odd = lax.rem(lat, 2)
    partner = lat + 1 - 2 * odd
    target = lat + 2 - 4 * odd
    source = lat - 2 + 4 * odd
    hands_on = jnp.logical_and(target >= 0, target < n_lat)
    gets = jnp.logical_and(source >= 0, source < n_lat)
    right, left = lax.rem(lon + 1, n_lon), lax.rem(lon + n_lon - 1, n_lon)
    far = 2 * size * odd
    near = 2 * size * (1 - odd)

    def plane_peer(o):
        peer = lax.rem(me + o, n_p)
        return peer, (peer // pair, z * pair + lax.rem(peer, pair))

    def z_peer(o):
        return (lat, lax.rem(z + o, n_z) * pair + core)

    barrier = pltpu.get_barrier_semaphore()
    for o in range(1, n_p):
        pl.semaphore_signal(barrier, inc=1, device_id=plane_peer(o)[1], device_id_type=MESH)
    for o in range(1, n_z):
        pl.semaphore_signal(barrier, inc=1, device_id=z_peer(o), device_id_type=MESH)
    for side_dev in (left, right):
        pl.semaphore_signal(barrier, inc=1, device_id=(lat, side_dev), device_id_type=MESH)

    def up(k):
        return k * step + odd * ((pieces - 1 - 2 * k) * step)

    def down(k):
        return (pieces - 1 - k) * step + odd * ((2 * k - pieces + 1) * step)

    def at(start):
        return pl.ds(pl.multiple_of(start, 8), step)

    def swap(c, k):
        return pltpu.make_async_remote_copy(
            src_ref=ext.at[c, at(size + up(k))], dst_ref=ext.at[c, at(far + up(k))],
            send_sem=psend.at[c, k], recv_sem=precv.at[c, k], device_id=(partner, lon), device_id_type=MESH)

    def hand(c, k):
        return pltpu.make_async_remote_copy(
            src_ref=ext.at[c, at(near + down(k))], dst_ref=ext.at[c, at(far + down(k))],
            send_sem=fsend.at[c, k], recv_sem=frecv.at[c, k], device_id=(target, lon), device_id_type=MESH)

    def side(c, k, way):
        start = up(k) if c else down(k)
        return pltpu.make_async_remote_copy(
            src_ref=lonb.at[c, 1, at(start)], dst_ref=lonb.at[c, 2 * way, at(start)],
            send_sem=lsend.at[c, k, way], recv_sem=lrecv.at[c, k, way],
            device_id=(lat, left if way else right), device_id_type=MESH)

    def relay(c, k):
        swap(c, k).wait_recv()

        @pl.when(hands_on)
        def _():
            hand(c, k).start()

    def lat_smooth(c, start):
        sums = {}
        for k in range(taps):
            place = (k + rows_lat - taps // 2) * cols
            q = place % 8
            rows = step + 8 if q else step
            value = lat_ref[k] * ext[c, pl.ds(pl.multiple_of(start + place - q, 8), rows)]
            sums[q] = sums[q] + value if q in sums else value
        return sum(v[q:q + step] for q, v in sums.items())

    def lon_smooth(c, start):
        value = jnp.concatenate([lonb[c, p, at(start)] for p in range(3)], axis=0)
        return jnp.dot(band_ref[...], value, precision=lax.Precision.HIGHEST, preferred_element_type=jnp.float32)

    def weighted(value, start):
        row = lat * rows_lat + start // cols
        place = lax.broadcasted_iota(jnp.int32, value.shape, 0)
        weight = jnp.zeros(value.shape, jnp.float32) + w_ref[row]
        for q in range(1, group):
            weight = jnp.where(place >= q * cols, w_ref[row + q], weight)
        return value * weight

    length = x_ref.shape[2]
    half = v_ref.shape[0]
    for i in range(rows_lat):
        flat[i * cols:(i + 1) * cols] = x_ref[i]
    lane = lax.broadcasted_iota(jnp.int32, (1, length), 1)
    row_ref[...] = jnp.zeros((1, length), jnp.float32)
    row_ref[:, :half] = v_ref[...].reshape(1, half)
    row = jnp.where(lane == half // 2, row_ref[...] + 1.0, row_ref[...])
    shifts = pltpu.roll(jnp.broadcast_to(row, (chunks * LANES, length)), 0, 1, stride=1, stride_axis=0)

    def filtered(c):
        return lax.dot_general(
            flat[...], shifts[c * LANES:(c + 1) * LANES], (((1,), (1,)), ((), ())),
            precision=lax.Precision.HIGHEST, preferred_element_type=jnp.float32)

    ext[0, size:2 * size] = filtered(0)
    pl.semaphore_wait(barrier, n_p + n_z)
    for k in range(pieces):
        swap(0, k).start()
    lonb[1, 1] = filtered(1)
    for k in range(pieces):
        side(1, k, 0).start()
        side(1, k, 1).start()

    @pl.when(jnp.logical_not(gets))
    def _():
        for c in range(chunks):
            ext[c, pl.ds(pl.multiple_of(far, 8), size)] = jnp.zeros((size, LANES), jnp.float32)

    parts = 3
    shape = (step, parts * step)
    r, e = lax.broadcasted_iota(jnp.int32, shape, 0), lax.broadcasted_iota(jnp.int32, shape, 1)
    part = sum((e >= p * step).astype(jnp.int32) for p in range(1, parts)) + jnp.zeros(shape, jnp.int32)
    e = e - part * step
    er = sum((e >= q * cols).astype(jnp.int32) for q in range(1, group)) + jnp.zeros(shape, jnp.int32)
    rr = sum((r >= q * cols).astype(jnp.int32) for q in range(1, group)) + jnp.zeros(shape, jnp.int32)
    offset = part * cols + (e - er * cols) - (r - rr * cols) - (cols - taps // 2)
    offset = jnp.where(er == rr, offset, -1)
    band = jnp.zeros(shape, jnp.float32)
    for k in range(taps):
        band = jnp.where(offset == k, lon_ref[k], band)
    band_ref[...] = band

    for k in range(pieces):
        relay(0, k)
        side(1, k, 0).wait_recv()
        side(1, k, 1).wait_recv()
        ext[1, at(size + up(k))] = lon_smooth(1, up(k))
        swap(1, k).start()
    for k in range(pieces):
        @pl.when(gets)
        def _():
            hand(0, k).wait_recv()

        lonb[0, 1, at(down(k))] = lat_smooth(0, down(k))
        side(0, k, 0).start()
        side(0, k, 1).start()
        relay(1, k)
    for k in range(pieces):
        side(0, k, 0).wait_recv()
        side(0, k, 1).wait_recv()
        m_ref[at(down(k)), :LANES] = weighted(lon_smooth(0, down(k)), down(k))
    for k in range(pieces):
        @pl.when(gets)
        def _():
            hand(1, k).wait_recv()

        m_ref[at(down(k)), LANES:] = weighted(lat_smooth(1, down(k)), down(k))

    steps = chunks * LANES
    place = 0
    for t in range(0, steps, LANES):
        both = lax.dot_general(
            m_ref[:, t:t + LANES], m_ref[:, t:], (((0,), (0,)), ((), ())),
            precision=lax.Precision.HIGHEST, preferred_element_type=jnp.float32)
        for q in range(0, steps - t, LANES):
            g_ref[place:place + LANES] = both[:, q:q + LANES]
            place += LANES

    copies = []
    for o in range(1, n_p):
        peer, dev = plane_peer(o)
        c = pltpu.make_async_remote_copy(
            src_ref=g_ref.at[pl.ds(pl.multiple_of(peer * share, 8), share)], dst_ref=rbuf.at[o],
            send_sem=ssem.at[o], recv_sem=rsem.at[o], device_id=dev, device_id_type=MESH)
        c.start()
        copies.append(c)
    for c in range(chunks):
        for k in range(pieces):
            swap(c, k).wait_send()
            side(c, k, 0).wait_send()
            side(c, k, 1).wait_send()

    @pl.when(hands_on)
    def _():
        for c in range(chunks):
            for k in range(pieces):
                hand(c, k).wait_send()

    mine = pl.ds(pl.multiple_of(me * share, 8), share)
    acc = g_ref[mine, :]
    for o in range(1, n_p):
        copies[o - 1].wait_recv()
        acc = acc + rbuf[o]
    for c in copies:
        c.wait_send()
    zbuf[z] = acc

    copies = []
    for o in range(1, n_z):
        c = pltpu.make_async_remote_copy(
            src_ref=zbuf.at[z], dst_ref=zbuf.at[z],
            send_sem=zssem.at[o], recv_sem=zrsem.at[o], device_id=z_peer(o), device_id_type=MESH)
        c.start()
        copies.append(c)
    for c in copies:
        c.wait()
    total = zbuf[0]
    for k in range(1, n_z):
        total = total + zbuf[k]
    out_ref[mine, :] = total

    copies = []
    for o in range(1, n_p):
        c = pltpu.make_async_remote_copy(
            src_ref=out_ref.at[mine], dst_ref=out_ref.at[mine],
            send_sem=cssem.at[o], recv_sem=crsem.at[o], device_id=plane_peer(o)[1], device_id_type=MESH)
        c.start()
        copies.append(c)
    for c in copies:
        c.wait()


def matrix_and_gram(field, time_taps, lat_kernel, lon_kernel, weights):
    rows_lat, cols, length = field.shape
    size = rows_lat * cols
    steps = length - time_taps.shape[0] + 1
    chunks = steps // LANES
    fits = [q for q in range(1, rows_lat + 1) if rows_lat % q == 0 and q * cols % 8 == 0]
    group = next((q for q in fits if q * cols >= 64), fits[-1])
    step = group * cols
    pieces = rows_lat // group
    packed = LANES * chunks * (chunks + 1) // 2
    n_lat, n_lon = lax.axis_size("lat"), lax.axis_size("lon")
    pair = 2 if n_lon % 2 == 0 else 1
    n_p, n_z = n_lat * pair, n_lon // pair
    share = packed // n_p
    dma = pltpu.SemaphoreType.DMA
    vmem, smem = pl.BlockSpec(memory_space=pltpu.VMEM), pl.BlockSpec(memory_space=pltpu.SMEM)
    return pl.pallas_call(
        functools.partial(front_kernel, n_lat, n_lon, pair, cols, group),
        out_shape=(jax.ShapeDtypeStruct((size, steps), jnp.float32), jax.ShapeDtypeStruct((packed, LANES), jnp.float32)),
        in_specs=[vmem, vmem, smem, smem, smem],
        out_specs=(vmem, vmem),
        scratch_shapes=[
            pltpu.VMEM((size, length), jnp.float32),
            pltpu.VMEM((1, length), jnp.float32),
            pltpu.VMEM((step, 3 * step), jnp.float32),
            pltpu.VMEM((chunks, 3 * size, LANES), jnp.float32),
            pltpu.VMEM((chunks, 3, size, LANES), jnp.float32),
            pltpu.VMEM((packed, LANES), jnp.float32),
            pltpu.VMEM((n_p, share, LANES), jnp.float32),
            pltpu.VMEM((n_z, share, LANES), jnp.float32),
        ] + [dma((chunks, pieces))] * 4 + [dma((chunks, pieces, 2))] * 2
        + [dma((n_p,)), dma((n_p,)), dma((n_z,)), dma((n_z,)), dma((n_p,)), dma((n_p,))],
        compiler_params=pltpu.CompilerParams(collective_id=0, has_side_effects=True),
        name="front",
    )(field, time_taps, lat_kernel, lon_kernel, weights)


def body(field, lat_kernel, lon_kernel, time_taps):
    rows_lat, rows_lon = field.shape[:2]
    total_lat = rows_lat * lax.axis_size("lat")
    cells = total_lat * rows_lon * lax.axis_size("lon")
    latitude = np.pi * (np.arange(total_lat) + 0.5) / total_lat - np.pi / 2
    weights = jnp.asarray(np.sqrt(np.cos(latitude)), jnp.float32)
    matrix, gram = matrix_and_gram(field, time_taps, lat_kernel, lon_kernel, weights)
    upper, basis = factor(gram, matrix, float(cells) ** 0.5, rows_lat, rows_lon)
    return (basis, upper)


def solution(mesh):
    placed = (P("lat", "lon", None), P(), P(), P())
    return jax.shard_map(
        body, mesh=mesh, in_specs=placed, out_specs=(P("lat", "lon", None), P()), check_vma=False
    )
```

```python
import functools

import jax
import jax.numpy as jnp
import numpy as np
from jax import lax
from jax.experimental import pallas as pl
from jax.experimental.pallas import tpu as pltpu
from jax.sharding import PartitionSpec as P


MESH = pl.DeviceIdType.MESH
NB = 64
LANES = 128


def spread(x, q):
    return jnp.broadcast_to(x[q:q + 1, :], (8, LANES))


def column(x, lane):
    return jnp.take_along_axis(x, jnp.full(x.shape, lane, jnp.int32), axis=1, mode="promise_in_bounds")


def eliminate(grp, first):
    sub = lax.broadcasted_iota(jnp.int32, (8, LANES), 0)
    tiles = range(len(grp[0]))
    for g in range(len(grp)):
        lane = first + 8 * g
        cols = [{h: column(grp[h][0], lane + q) for h in range(g, len(grp))} for q in range(8)]
        s = {(i, j): spread(cols[j][g], i) for j in range(8) for i in range(j, 8)}
        rows = [[spread(grp[g][t], q) for t in tiles] for q in range(8)]
        inv, low, pivots = [None] * 8, {}, None
        for q in range(8):
            if q % 2 == 0:
                inv[q] = pltpu.reciprocal(s[q, q])
                inv[q + 1] = s[q, q] * pltpu.reciprocal(s[q, q] * s[q + 1, q + 1] - s[q + 1, q] * s[q + 1, q])
            pivots = s[q, q] if pivots is None else jnp.where(sub == q, s[q, q], pivots)
            for i in range(q + 1, 8):
                low[i, q] = s[i, q] * inv[q]
            for j in range(q + 1, 8):
                for i in range(j, 8):
                    s[i, j] = s[i, j] - low[i, q] * s[j, q]
        for q in range(8):
            for p in range(q + 1, 8):
                for t in tiles:
                    rows[p][t] = rows[p][t] - low[p, q] * rows[q][t]
        for h in range(g + 1, len(grp)):
            for q in range(8):
                u = cols[q][h] * inv[q]
                for p in range(q + 1, 8):
                    cols[p][h] = cols[p][h] - u * s[p, q]
                for t in tiles:
                    grp[h][t] = grp[h][t] - u * rows[q][t]
        rinv = lax.rsqrt(pivots)
        for t in tiles:
            done = rows[0][t]
            for q in range(1, 8):
                done = jnp.where(sub == q, rows[q][t], done)
            grp[g][t] = done * rinv


def factor_kernel(scale, n, g_ref, m_ref, r_ref, basis_ref, a, b, y_ref):
    at = 0
    first = column(spread(g_ref[0:8], 0), 0)[0:1, :]
    unit = 1.0 / first
    for t in range(0, n, LANES):
        if t:
            a[t:t + LANES, :t] = jnp.zeros((LANES, t), jnp.float32)
        for q in range(t, n, LANES):
            a[t:t + LANES, q:q + LANES] = g_ref[at:at + LANES] * unit
            at += LANES
    root = lax.sqrt(first)[:, :1]
    to_r = root / scale
    to_y = scale / root
    b[...] = (lax.broadcasted_iota(jnp.int32, (n, n), 0) == lax.broadcasted_iota(jnp.int32, (n, n), 1)).astype(jnp.float32)
    tiles = n // LANES
    for k in range(0, n, NB):
        kt = k // LANES
        live = [(a, t) for t in range(kt, tiles)] + [(b, t) for t in range(kt + 1)]
        grp = [[ref[k + 8 * h:k + 8 * h + 8, t * LANES:(t + 1) * LANES] for ref, t in live] for h in range(NB // 8)]
        eliminate(grp, k - kt * LANES)
        panel = jnp.concatenate([jnp.concatenate(x, axis=1) for x in grp], axis=0)
        n_a = tiles - kt
        row_id = lax.broadcasted_iota(jnp.int32, (NB, n_a * LANES), 0) + k
        lane_id = lax.broadcasted_iota(jnp.int32, (NB, n_a * LANES), 1) + kt * LANES
        pa = panel[:, :n_a * LANES]
        pb = panel[:, n_a * LANES:]
        if kt:
            r_ref[k:k + NB, :kt * LANES] = jnp.zeros((NB, kt * LANES), jnp.float32)
        r_ref[k:k + NB, kt * LANES:] = jnp.where(lane_id >= row_id, pa * to_r, 0.0)
        y_ref[k:k + NB, :(kt + 1) * LANES] = pb * to_y
        if kt + 1 < tiles:
            y_ref[k:k + NB, (kt + 1) * LANES:] = jnp.zeros((NB, n - (kt + 1) * LANES), jnp.float32)
        nxt = k + NB
        if nxt < n:
            nt = nxt // LANES
            left = panel[:, (nt - kt) * LANES:n_a * LANES]
            dims = (((0,), (0,)), ((), ()))
            right = panel[:, (nt - kt) * LANES:]
            upd = lax.dot_general(left, right, dims, precision=lax.Precision.HIGHEST, preferred_element_type=jnp.float32)
            upd = upd[nxt - nt * LANES:]
            w_a = n - nt * LANES
            a[nxt:, nt * LANES:] = a[nxt:, nt * LANES:] - upd[:, :w_a]
            b[nxt:, :(kt + 1) * LANES] = b[nxt:, :(kt + 1) * LANES] - upd[:, w_a:]
        if nxt % LANES == 0:
            at = kt * LANES
            part = lax.dot_general(
                m_ref[:, :nxt], y_ref[at:nxt, :nxt], (((1,), (1,)), ((), ())),
                precision=lax.Precision.HIGHEST, preferred_element_type=jnp.float32)
            cols = basis_ref.shape[1]
            for i in range(basis_ref.shape[0]):
                basis_ref[i, :, at:nxt] = part[i * cols:(i + 1) * cols]


def factor(gram, matrix, scale, rows, cols):
    n = matrix.shape[1]
    square = jax.ShapeDtypeStruct((n, n), jnp.float32)
    vmem = pl.BlockSpec(memory_space=pltpu.VMEM)
    return pl.pallas_call(
        functools.partial(factor_kernel, scale, n),
        out_shape=(square, jax.ShapeDtypeStruct((rows, cols, n), jnp.float32)),
        in_specs=[vmem, vmem],
        out_specs=(vmem, vmem),
        scratch_shapes=[pltpu.VMEM((n, n), jnp.float32)] * 3,
        name="factor",
    )(gram, matrix)


def front_kernel(n_lat, n_lon, pair, cols, group, x_ref, v_ref, lat_ref, lon_ref, w_ref, m_ref, out_ref, flat, row_ref, band_ref, ext, lonb, g_ref, rbuf, zbuf, psend, precv, fsend, frecv, lsend, lrecv, ssem, rsem, zssem, zrsem, cssem, crsem):
    lat, lon = lax.axis_index("lat"), lax.axis_index("lon")
    n_p, n_z = n_lat * pair, n_lon // pair
    share = g_ref.shape[0] // n_p
    core, z = lax.rem(lon, pair), lon // pair
    me = lat * pair + core
    chunks, size = lonb.shape[0], lonb.shape[2]
    rows_lat = size // cols
    taps = lat_ref.shape[0]
    step = group * cols
    pieces = size // step
    odd = lax.rem(lat, 2)
    partner = lat + 1 - 2 * odd
    target = lat + 2 - 4 * odd
    source = lat - 2 + 4 * odd
    hands_on = jnp.logical_and(target >= 0, target < n_lat)
    gets = jnp.logical_and(source >= 0, source < n_lat)
    right, left = lax.rem(lon + 1, n_lon), lax.rem(lon + n_lon - 1, n_lon)
    far = 2 * size * odd
    near = 2 * size * (1 - odd)

    def plane_peer(o):
        peer = lax.rem(me + o, n_p)
        return peer, (peer // pair, z * pair + lax.rem(peer, pair))

    def z_peer(o):
        return (lat, lax.rem(z + o, n_z) * pair + core)

    barrier = pltpu.get_barrier_semaphore()
    for o in range(1, n_p):
        pl.semaphore_signal(barrier, inc=1, device_id=plane_peer(o)[1], device_id_type=MESH)
    for o in range(1, n_z):
        pl.semaphore_signal(barrier, inc=1, device_id=z_peer(o), device_id_type=MESH)
    for side_dev in (left, right):
        pl.semaphore_signal(barrier, inc=1, device_id=(lat, side_dev), device_id_type=MESH)

    def up(k):
        return k * step + odd * ((pieces - 1 - 2 * k) * step)

    def down(k):
        return (pieces - 1 - k) * step + odd * ((2 * k - pieces + 1) * step)

    def at(start):
        return pl.ds(pl.multiple_of(start, 8), step)

    def swap(c, k):
        return pltpu.make_async_remote_copy(
            src_ref=ext.at[c, at(size + up(k))], dst_ref=ext.at[c, at(far + up(k))],
            send_sem=psend.at[c, k], recv_sem=precv.at[c, k], device_id=(partner, lon), device_id_type=MESH)

    def hand(c, k):
        return pltpu.make_async_remote_copy(
            src_ref=ext.at[c, at(near + down(k))], dst_ref=ext.at[c, at(far + down(k))],
            send_sem=fsend.at[c, k], recv_sem=frecv.at[c, k], device_id=(target, lon), device_id_type=MESH)

    def side(c, k, way):
        start = up(k) if c else down(k)
        return pltpu.make_async_remote_copy(
            src_ref=lonb.at[c, 1, at(start)], dst_ref=lonb.at[c, 2 * way, at(start)],
            send_sem=lsend.at[c, k, way], recv_sem=lrecv.at[c, k, way],
            device_id=(lat, left if way else right), device_id_type=MESH)

    def relay(c, k):
        swap(c, k).wait_recv()

        @pl.when(hands_on)
        def _():
            hand(c, k).start()

    def lat_smooth(c, start):
        sums = {}
        for k in range(taps):
            place = (k + rows_lat - taps // 2) * cols
            q = place % 8
            rows = step + 8 if q else step
            value = lat_ref[k] * ext[c, pl.ds(pl.multiple_of(start + place - q, 8), rows)]
            sums[q] = sums[q] + value if q in sums else value
        return sum(v[q:q + step] for q, v in sums.items())

    def lon_smooth(c, start):
        value = jnp.concatenate([lonb[c, p, at(start)] for p in range(3)], axis=0)
        return jnp.dot(band_ref[...], value, precision=lax.Precision.HIGHEST, preferred_element_type=jnp.float32)

    def weighted(value, start):
        row = lat * rows_lat + start // cols
        place = lax.broadcasted_iota(jnp.int32, value.shape, 0)
        weight = jnp.zeros(value.shape, jnp.float32) + w_ref[row]
        for q in range(1, group):
            weight = jnp.where(place >= q * cols, w_ref[row + q], weight)
        return value * weight

    length = x_ref.shape[2]
    half = v_ref.shape[0]
    for i in range(rows_lat):
        flat[i * cols:(i + 1) * cols] = x_ref[i]
    lane = lax.broadcasted_iota(jnp.int32, (1, length), 1)
    row_ref[...] = jnp.zeros((1, length), jnp.float32)
    row_ref[:, :half] = v_ref[...].reshape(1, half)
    row = jnp.where(lane == half // 2, row_ref[...] + 1.0, row_ref[...])
    shifts = pltpu.roll(jnp.broadcast_to(row, (chunks * LANES, length)), 0, 1, stride=1, stride_axis=0)

    def filtered(c):
        return lax.dot_general(
            flat[...], shifts[c * LANES:(c + 1) * LANES], (((1,), (1,)), ((), ())),
            precision=lax.Precision.HIGHEST, preferred_element_type=jnp.float32)

    ext[0, size:2 * size] = filtered(0)
    pl.semaphore_wait(barrier, n_p + n_z)
    for k in range(pieces):
        swap(0, k).start()
    lonb[1, 1] = filtered(1)
    for k in range(pieces):
        side(1, k, 0).start()
        side(1, k, 1).start()

    @pl.when(jnp.logical_not(gets))
    def _():
        for c in range(chunks):
            ext[c, pl.ds(pl.multiple_of(far, 8), size)] = jnp.zeros((size, LANES), jnp.float32)

    parts = 3
    shape = (step, parts * step)
    r, e = lax.broadcasted_iota(jnp.int32, shape, 0), lax.broadcasted_iota(jnp.int32, shape, 1)
    part = sum((e >= p * step).astype(jnp.int32) for p in range(1, parts)) + jnp.zeros(shape, jnp.int32)
    e = e - part * step
    er = sum((e >= q * cols).astype(jnp.int32) for q in range(1, group)) + jnp.zeros(shape, jnp.int32)
    rr = sum((r >= q * cols).astype(jnp.int32) for q in range(1, group)) + jnp.zeros(shape, jnp.int32)
    offset = part * cols + (e - er * cols) - (r - rr * cols) - (cols - taps // 2)
    offset = jnp.where(er == rr, offset, -1)
    band = jnp.zeros(shape, jnp.float32)
    for k in range(taps):
        band = jnp.where(offset == k, lon_ref[k], band)
    band_ref[...] = band

    def lon_first(k):
        side(1, k, 0).wait_recv()
        side(1, k, 1).wait_recv()
        ext[1, at(size + up(k))] = lon_smooth(1, up(k))
        swap(1, k).start()

    def lat_first(k):
        @pl.when(gets)
        def _():
            hand(0, k).wait_recv()

        lonb[0, 1, at(down(k))] = lat_smooth(0, down(k))
        side(0, k, 0).start()
        side(0, k, 1).start()

    def lon_last(k):
        side(0, k, 0).wait_recv()
        side(0, k, 1).wait_recv()
        m_ref[at(down(k)), :LANES] = weighted(lon_smooth(0, down(k)), down(k))

    def lat_last(k):
        @pl.when(gets)
        def _():
            hand(1, k).wait_recv()

        m_ref[at(down(k)), LANES:] = weighted(lat_smooth(1, down(k)), down(k))

    relay_0, relay_1 = functools.partial(relay, 0), functools.partial(relay, 1)
    order = [(k, relay_0, k) for k in range(pieces)]
    order += [(k + 1.5, lon_first, k) for k in range(pieces)]
    order += [(pieces - 0.8 + k, lat_first, k) for k in range(pieces)]
    order += [(pieces + 2.5 + k, relay_1, k) for k in range(pieces)]
    order += [(3 * pieces + k, lon_last, k) for k in range(pieces)]
    order += [(3 * pieces + k + 0.5, lat_last, k) for k in range(pieces)]
    for _, do, k in sorted(order, key=lambda item: item[0]):
        do(k)

    steps = chunks * LANES
    place = 0
    for t in range(0, steps, LANES):
        both = lax.dot_general(
            m_ref[:, t:t + LANES], m_ref[:, t:], (((0,), (0,)), ((), ())),
            precision=lax.Precision.HIGHEST, preferred_element_type=jnp.float32)
        for q in range(0, steps - t, LANES):
            g_ref[place:place + LANES] = both[:, q:q + LANES]
            place += LANES

    copies = []
    for o in range(1, n_p):
        peer, dev = plane_peer(o)
        c = pltpu.make_async_remote_copy(
            src_ref=g_ref.at[pl.ds(pl.multiple_of(peer * share, 8), share)], dst_ref=rbuf.at[o],
            send_sem=ssem.at[o], recv_sem=rsem.at[o], device_id=dev, device_id_type=MESH)
        c.start()
        copies.append(c)
    for c in range(chunks):
        for k in range(pieces):
            swap(c, k).wait_send()
            side(c, k, 0).wait_send()
            side(c, k, 1).wait_send()

    @pl.when(hands_on)
    def _():
        for c in range(chunks):
            for k in range(pieces):
                hand(c, k).wait_send()

    mine = pl.ds(pl.multiple_of(me * share, 8), share)
    acc = g_ref[mine, :]
    for o in range(1, n_p):
        copies[o - 1].wait_recv()
        acc = acc + rbuf[o]
    for c in copies:
        c.wait_send()
    zbuf[z] = acc

    copies = []
    for o in range(1, n_z):
        c = pltpu.make_async_remote_copy(
            src_ref=zbuf.at[z], dst_ref=zbuf.at[z],
            send_sem=zssem.at[o], recv_sem=zrsem.at[o], device_id=z_peer(o), device_id_type=MESH)
        c.start()
        copies.append(c)
    for c in copies:
        c.wait()
    total = zbuf[0]
    for k in range(1, n_z):
        total = total + zbuf[k]
    out_ref[mine, :] = total

    copies = []
    for o in range(1, n_p):
        c = pltpu.make_async_remote_copy(
            src_ref=out_ref.at[mine], dst_ref=out_ref.at[mine],
            send_sem=cssem.at[o], recv_sem=crsem.at[o], device_id=plane_peer(o)[1], device_id_type=MESH)
        c.start()
        copies.append(c)
    for c in copies:
        c.wait()


def matrix_and_gram(field, time_taps, lat_kernel, lon_kernel, weights):
    rows_lat, cols, length = field.shape
    size = rows_lat * cols
    steps = length - time_taps.shape[0] + 1
    chunks = steps // LANES
    fits = [q for q in range(1, rows_lat + 1) if rows_lat % q == 0 and q * cols % 8 == 0]
    group = next((q for q in fits if q * cols >= 64), fits[-1])
    step = group * cols
    pieces = rows_lat // group
    packed = LANES * chunks * (chunks + 1) // 2
    n_lat, n_lon = lax.axis_size("lat"), lax.axis_size("lon")
    pair = 2 if n_lon % 2 == 0 else 1
    n_p, n_z = n_lat * pair, n_lon // pair
    share = packed // n_p
    dma = pltpu.SemaphoreType.DMA
    vmem, smem = pl.BlockSpec(memory_space=pltpu.VMEM), pl.BlockSpec(memory_space=pltpu.SMEM)
    return pl.pallas_call(
        functools.partial(front_kernel, n_lat, n_lon, pair, cols, group),
        out_shape=(jax.ShapeDtypeStruct((size, steps), jnp.float32), jax.ShapeDtypeStruct((packed, LANES), jnp.float32)),
        in_specs=[vmem, vmem, smem, smem, smem],
        out_specs=(vmem, vmem),
        scratch_shapes=[
            pltpu.VMEM((size, length), jnp.float32),
            pltpu.VMEM((1, length), jnp.float32),
            pltpu.VMEM((step, 3 * step), jnp.float32),
            pltpu.VMEM((chunks, 3 * size, LANES), jnp.float32),
            pltpu.VMEM((chunks, 3, size, LANES), jnp.float32),
            pltpu.VMEM((packed, LANES), jnp.float32),
            pltpu.VMEM((n_p, share, LANES), jnp.float32),
            pltpu.VMEM((n_z, share, LANES), jnp.float32),
        ] + [dma((chunks, pieces))] * 4 + [dma((chunks, pieces, 2))] * 2
        + [dma((n_p,)), dma((n_p,)), dma((n_z,)), dma((n_z,)), dma((n_p,)), dma((n_p,))],
        compiler_params=pltpu.CompilerParams(collective_id=0, has_side_effects=True),
        name="front",
    )(field, time_taps, lat_kernel, lon_kernel, weights)


def body(field, lat_kernel, lon_kernel, time_taps):
    rows_lat, rows_lon = field.shape[:2]
    total_lat = rows_lat * lax.axis_size("lat")
    cells = total_lat * rows_lon * lax.axis_size("lon")
    latitude = np.pi * (np.arange(total_lat) + 0.5) / total_lat - np.pi / 2
    weights = jnp.asarray(np.sqrt(np.cos(latitude)), jnp.float32)
    matrix, gram = matrix_and_gram(field, time_taps, lat_kernel, lon_kernel, weights)
    upper, basis = factor(gram, matrix, float(cells) ** 0.5, rows_lat, rows_lon)
    return (basis, upper)


def solution(mesh):
    placed = (P("lat", "lon", None), P(), P(), P())
    return jax.shard_map(
        body, mesh=mesh, in_specs=placed, out_specs=(P("lat", "lon", None), P()), check_vma=False
    )
```

```python
import functools

import jax
import jax.numpy as jnp
import numpy as np
from jax import lax
from jax.experimental import pallas as pl
from jax.experimental.pallas import tpu as pltpu
from jax.sharding import PartitionSpec as P


MESH = pl.DeviceIdType.MESH
NB = 64
LANES = 128
HALF = LANES // 2


def spread(x, q):
    return jnp.broadcast_to(x[q:q + 1, :], (8, LANES))


def column(x, lane):
    return jnp.take_along_axis(x, jnp.full(x.shape, lane, jnp.int32), axis=1, mode="promise_in_bounds")


def eliminate(grp, first):
    sub = lax.broadcasted_iota(jnp.int32, (8, LANES), 0)
    tiles = range(len(grp[0]))
    for g in range(len(grp)):
        lane = first + 8 * g
        cols = [{h: column(grp[h][0], lane + q) for h in range(g, len(grp))} for q in range(8)]
        s = {(i, j): spread(cols[j][g], i) for j in range(8) for i in range(j, 8)}
        rows = [[spread(grp[g][t], q) for t in tiles] for q in range(8)]
        inv, low, pivots = [None] * 8, {}, None
        for q in range(8):
            if q % 2 == 0:
                inv[q] = pltpu.reciprocal(s[q, q])
                inv[q + 1] = s[q, q] * pltpu.reciprocal(s[q, q] * s[q + 1, q + 1] - s[q + 1, q] * s[q + 1, q])
            pivots = s[q, q] if pivots is None else jnp.where(sub == q, s[q, q], pivots)
            for i in range(q + 1, 8):
                low[i, q] = s[i, q] * inv[q]
            for j in range(q + 1, 8):
                for i in range(j, 8):
                    s[i, j] = s[i, j] - low[i, q] * s[j, q]
        for q in range(8):
            for p in range(q + 1, 8):
                for t in tiles:
                    rows[p][t] = rows[p][t] - low[p, q] * rows[q][t]
        for h in range(g + 1, len(grp)):
            for q in range(8):
                u = cols[q][h] * inv[q]
                for p in range(q + 1, 8):
                    cols[p][h] = cols[p][h] - u * s[p, q]
                for t in tiles:
                    grp[h][t] = grp[h][t] - u * rows[q][t]
        rinv = lax.rsqrt(pivots)
        for t in tiles:
            done = rows[0][t]
            for q in range(1, 8):
                done = jnp.where(sub == q, rows[q][t], done)
            grp[g][t] = done * rinv


def factor_kernel(scale, n, g_ref, m_ref, r_ref, basis_ref, a, b, y_ref):
    at = 0
    first = column(spread(g_ref[0:8], 0), 0)[0:1, :]
    unit = 1.0 / first
    tiles = n // LANES
    tails = []
    for t in range(tiles):
        if t:
            a[t * LANES:(t + 1) * LANES, :t * LANES] = jnp.zeros((LANES, t * LANES), jnp.float32)
        for r in range(2):
            row = t * LANES + r * HALF
            for q in range(t + r, tiles):
                a[row:row + HALF, q * LANES:(q + 1) * LANES] = g_ref[at:at + HALF] * unit
                at += HALF
        tails.append(t)
        if len(tails) == 2 or t == tiles - 1:
            both = g_ref[at:at + HALF] * unit
            at += HALF
            lane = lax.broadcasted_iota(jnp.int32, both.shape, 1)
            for u in tails:
                tail = both if u % 2 or len(tails) == 1 else pltpu.roll(both, HALF, 1)
                a[u * LANES + HALF:(u + 1) * LANES, u * LANES:(u + 1) * LANES] = jnp.where(lane < HALF, 0.0, tail)
            tails = []
    root = lax.sqrt(first)[:, :1]
    to_r = root / scale
    to_y = scale / root
    b[...] = (lax.broadcasted_iota(jnp.int32, (n, n), 0) == lax.broadcasted_iota(jnp.int32, (n, n), 1)).astype(jnp.float32)
    for k in range(0, n, NB):
        kt = k // LANES
        live = [(a, t) for t in range(kt, tiles)] + [(b, t) for t in range(kt + 1)]
        grp = [[ref[k + 8 * h:k + 8 * h + 8, t * LANES:(t + 1) * LANES] for ref, t in live] for h in range(NB // 8)]
        eliminate(grp, k - kt * LANES)
        panel = jnp.concatenate([jnp.concatenate(x, axis=1) for x in grp], axis=0)
        n_a = tiles - kt
        row_id = lax.broadcasted_iota(jnp.int32, (NB, n_a * LANES), 0) + k
        lane_id = lax.broadcasted_iota(jnp.int32, (NB, n_a * LANES), 1) + kt * LANES
        pa = panel[:, :n_a * LANES]
        pb = panel[:, n_a * LANES:]
        if kt:
            r_ref[k:k + NB, :kt * LANES] = jnp.zeros((NB, kt * LANES), jnp.float32)
        r_ref[k:k + NB, kt * LANES:] = jnp.where(lane_id >= row_id, pa * to_r, 0.0)
        y_ref[k:k + NB, :(kt + 1) * LANES] = pb * to_y
        if kt + 1 < tiles:
            y_ref[k:k + NB, (kt + 1) * LANES:] = jnp.zeros((NB, n - (kt + 1) * LANES), jnp.float32)
        nxt = k + NB
        if nxt < n:
            nt = nxt // LANES
            left = panel[:, (nt - kt) * LANES:n_a * LANES]
            dims = (((0,), (0,)), ((), ()))
            right = panel[:, (nt - kt) * LANES:]
            upd = lax.dot_general(left, right, dims, precision=lax.Precision.HIGHEST, preferred_element_type=jnp.float32)
            upd = upd[nxt - nt * LANES:]
            w_a = n - nt * LANES
            a[nxt:, nt * LANES:] = a[nxt:, nt * LANES:] - upd[:, :w_a]
            b[nxt:, :(kt + 1) * LANES] = b[nxt:, :(kt + 1) * LANES] - upd[:, w_a:]
        if nxt % LANES == 0:
            at = kt * LANES
            part = lax.dot_general(
                m_ref[:, :nxt], y_ref[at:nxt, :nxt], (((1,), (1,)), ((), ())),
                precision=lax.Precision.HIGHEST, preferred_element_type=jnp.float32)
            cols = basis_ref.shape[1]
            for i in range(basis_ref.shape[0]):
                basis_ref[i, :, at:nxt] = part[i * cols:(i + 1) * cols]


def factor(gram, matrix, scale, rows, cols):
    n = matrix.shape[1]
    square = jax.ShapeDtypeStruct((n, n), jnp.float32)
    vmem = pl.BlockSpec(memory_space=pltpu.VMEM)
    return pl.pallas_call(
        functools.partial(factor_kernel, scale, n),
        out_shape=(square, jax.ShapeDtypeStruct((rows, cols, n), jnp.float32)),
        in_specs=[vmem, vmem],
        out_specs=(vmem, vmem),
        scratch_shapes=[pltpu.VMEM((n, n), jnp.float32)] * 3,
        name="factor",
    )(gram, matrix)


def front_kernel(n_lat, n_lon, pair, cols, group, x_ref, v_ref, lat_ref, lon_ref, w_ref, m_ref, out_ref, flat, row_ref, band_ref, ext, lonb, g_ref, rbuf, zbuf, psend, precv, fsend, frecv, lsend, lrecv, ssem, rsem, zssem, zrsem, cssem, crsem):
    lat, lon = lax.axis_index("lat"), lax.axis_index("lon")
    n_p, n_z = n_lat * pair, n_lon // pair
    share = g_ref.shape[0] // n_p
    core, z = lax.rem(lon, pair), lon // pair
    me = lat * pair + core
    chunks, size = lonb.shape[0], lonb.shape[2]
    rows_lat = size // cols
    taps = lat_ref.shape[0]
    step = group * cols
    pieces = size // step
    odd = lax.rem(lat, 2)
    partner = lat + 1 - 2 * odd
    target = lat + 2 - 4 * odd
    source = lat - 2 + 4 * odd
    hands_on = jnp.logical_and(target >= 0, target < n_lat)
    gets = jnp.logical_and(source >= 0, source < n_lat)
    right, left = lax.rem(lon + 1, n_lon), lax.rem(lon + n_lon - 1, n_lon)
    far = 2 * size * odd
    near = 2 * size * (1 - odd)

    def plane_peer(o):
        peer = lax.rem(me + o, n_p)
        return peer, (peer // pair, z * pair + lax.rem(peer, pair))

    def z_peer(o):
        return (lat, lax.rem(z + o, n_z) * pair + core)

    barrier = pltpu.get_barrier_semaphore()
    for o in range(1, n_p):
        pl.semaphore_signal(barrier, inc=1, device_id=plane_peer(o)[1], device_id_type=MESH)
    for o in range(1, n_z):
        pl.semaphore_signal(barrier, inc=1, device_id=z_peer(o), device_id_type=MESH)
    for side_dev in (left, right):
        pl.semaphore_signal(barrier, inc=1, device_id=(lat, side_dev), device_id_type=MESH)

    def up(k):
        return k * step + odd * ((pieces - 1 - 2 * k) * step)

    def down(k):
        return (pieces - 1 - k) * step + odd * ((2 * k - pieces + 1) * step)

    def at(start):
        return pl.ds(pl.multiple_of(start, 8), step)

    def swap(c, k):
        return pltpu.make_async_remote_copy(
            src_ref=ext.at[c, at(size + up(k))], dst_ref=ext.at[c, at(far + up(k))],
            send_sem=psend.at[c, k], recv_sem=precv.at[c, k], device_id=(partner, lon), device_id_type=MESH)

    def hand(c, k):
        return pltpu.make_async_remote_copy(
            src_ref=ext.at[c, at(near + down(k))], dst_ref=ext.at[c, at(far + down(k))],
            send_sem=fsend.at[c, k], recv_sem=frecv.at[c, k], device_id=(target, lon), device_id_type=MESH)

    def side(c, k, way):
        start = up(k) if c else down(k)
        return pltpu.make_async_remote_copy(
            src_ref=lonb.at[c, 1, at(start)], dst_ref=lonb.at[c, 2 * way, at(start)],
            send_sem=lsend.at[c, k, way], recv_sem=lrecv.at[c, k, way],
            device_id=(lat, left if way else right), device_id_type=MESH)

    def relay(c, k):
        swap(c, k).wait_recv()

        @pl.when(hands_on)
        def _():
            hand(c, k).start()

    def lat_smooth(c, start):
        sums = {}
        for k in range(taps):
            place = (k + rows_lat - taps // 2) * cols
            q = place % 8
            rows = step + 8 if q else step
            value = lat_ref[k] * ext[c, pl.ds(pl.multiple_of(start + place - q, 8), rows)]
            sums[q] = sums[q] + value if q in sums else value
        return sum(v[q:q + step] for q, v in sums.items())

    def lon_smooth(c, start):
        value = jnp.concatenate([lonb[c, p, at(start)] for p in range(3)], axis=0)
        return jnp.dot(band_ref[...], value, precision=lax.Precision.HIGHEST, preferred_element_type=jnp.float32)

    def weighted(value, start):
        row = lat * rows_lat + start // cols
        place = lax.broadcasted_iota(jnp.int32, value.shape, 0)
        weight = jnp.zeros(value.shape, jnp.float32) + w_ref[row]
        for q in range(1, group):
            weight = jnp.where(place >= q * cols, w_ref[row + q], weight)
        return value * weight

    length = x_ref.shape[2]
    half = v_ref.shape[0]
    for i in range(rows_lat):
        flat[i * cols:(i + 1) * cols] = x_ref[i]
    span = row_ref.shape[1]
    lane = lax.broadcasted_iota(jnp.int32, (1, span), 1)
    row_ref[...] = jnp.zeros((1, span), jnp.float32)
    row_ref[:, :half] = v_ref[...].reshape(1, half)
    row = jnp.where(lane == half // 2, row_ref[...] + 1.0, row_ref[...])
    shifts = pltpu.roll(jnp.broadcast_to(row, (LANES, span)), 0, 1, stride=1, stride_axis=0)

    def filtered(c):
        return lax.dot_general(
            flat[:, c * LANES:c * LANES + span], shifts, (((1,), (1,)), ((), ())),
            precision=lax.Precision.HIGHEST, preferred_element_type=jnp.float32)

    ext[0, size:2 * size] = filtered(0)
    pl.semaphore_wait(barrier, n_p + n_z)
    for k in range(pieces):
        swap(0, k).start()
    lonb[1, 1] = filtered(1)
    for k in range(pieces):
        side(1, k, 0).start()
        side(1, k, 1).start()

    @pl.when(jnp.logical_not(gets))
    def _():
        for c in range(chunks):
            ext[c, pl.ds(pl.multiple_of(far, 8), size)] = jnp.zeros((size, LANES), jnp.float32)

    bands = 3
    shape = (step, bands * step)
    r, e = lax.broadcasted_iota(jnp.int32, shape, 0), lax.broadcasted_iota(jnp.int32, shape, 1)
    part = sum((e >= p * step).astype(jnp.int32) for p in range(1, bands)) + jnp.zeros(shape, jnp.int32)
    e = e - part * step
    er = sum((e >= q * cols).astype(jnp.int32) for q in range(1, group)) + jnp.zeros(shape, jnp.int32)
    rr = sum((r >= q * cols).astype(jnp.int32) for q in range(1, group)) + jnp.zeros(shape, jnp.int32)
    offset = part * cols + (e - er * cols) - (r - rr * cols) - (cols - taps // 2)
    offset = jnp.where(er == rr, offset, -1)
    band = jnp.zeros(shape, jnp.float32)
    for k in range(taps):
        band = jnp.where(offset == k, lon_ref[k], band)
    band_ref[...] = band

    def lon_first(k):
        side(1, k, 0).wait_recv()
        side(1, k, 1).wait_recv()
        ext[1, at(size + up(k))] = lon_smooth(1, up(k))
        swap(1, k).start()

    def lat_first(k):
        @pl.when(gets)
        def _():
            hand(0, k).wait_recv()

        lonb[0, 1, at(down(k))] = lat_smooth(0, down(k))
        side(0, k, 0).start()
        side(0, k, 1).start()

    def lon_last(k):
        side(0, k, 0).wait_recv()
        side(0, k, 1).wait_recv()
        m_ref[at(down(k)), :LANES] = weighted(lon_smooth(0, down(k)), down(k))

    def lat_last(k):
        @pl.when(gets)
        def _():
            hand(1, k).wait_recv()

        m_ref[at(down(k)), LANES:] = weighted(lat_smooth(1, down(k)), down(k))

    relay_0, relay_1 = functools.partial(relay, 0), functools.partial(relay, 1)
    order = [(k, relay_0, k) for k in range(pieces)]
    order += [(k + 1.5, lon_first, k) for k in range(pieces)]
    order += [(pieces - 0.8 + k, lat_first, k) for k in range(pieces)]
    order += [(pieces + 2.5 + k, relay_1, k) for k in range(pieces)]
    order += [(3 * pieces + k, lon_last, k) for k in range(pieces)]
    order += [(3 * pieces + k + 0.5, lat_last, k) for k in range(pieces)]
    for _, do, k in sorted(order, key=lambda item: item[0]):
        do(k)

    def mine(part, who):
        base, _, rows = part
        return pl.ds(pl.multiple_of(base + who * rows, 8), rows)

    def held(part):
        return pl.ds(part[1], part[2])

    def scatter(j):
        copies = []
        for o in range(1, n_p):
            peer, dev = plane_peer(o)
            c = pltpu.make_async_remote_copy(
                src_ref=g_ref.at[mine(parts[j], peer)], dst_ref=rbuf.at[o, held(parts[j])],
                send_sem=ssem.at[j, o], recv_sem=rsem.at[j, o], device_id=dev, device_id_type=MESH)
            c.start()
            copies.append(c)
        return copies

    parts = split_rows(share, n_p)
    sent = []
    place = 0
    tails = []
    for t in range(chunks):
        both = lax.dot_general(
            m_ref[:, t * LANES:(t + 1) * LANES], m_ref[:, t * LANES:], (((0,), (0,)), ((), ())),
            precision=lax.Precision.HIGHEST, preferred_element_type=jnp.float32)
        for r in range(2):
            for q in range(r, chunks - t):
                g_ref[place:place + HALF] = both[r * HALF:(r + 1) * HALF, q * LANES:(q + 1) * LANES]
                place += HALF
        tails.append(both[HALF:, :LANES])
        if len(tails) == 2 or t == chunks - 1:
            g_ref[place:place + HALF] = merge(tails[0], tails[-1])
            place += HALF
            tails = []
        if t == chunks - 1 and place < g_ref.shape[0]:
            g_ref[place:] = jnp.zeros((g_ref.shape[0] - place, LANES), jnp.float32)
            place = g_ref.shape[0]
        while len(sent) < len(parts) and parts[len(sent)][0] + n_p * parts[len(sent)][2] <= place:
            sent.append(scatter(len(sent)))

    for c in range(chunks):
        for k in range(pieces):
            swap(c, k).wait_send()
            side(c, k, 0).wait_send()
            side(c, k, 1).wait_send()

    @pl.when(hands_on)
    def _():
        for c in range(chunks):
            for k in range(pieces):
                hand(c, k).wait_send()

    along, back = [], []
    for j, part in enumerate(parts):
        acc = g_ref[mine(part, me), :]
        for o in range(1, n_p):
            sent[j][o - 1].wait_recv()
            acc = acc + rbuf[o, held(part)]
        zbuf[z, held(part)] = acc
        copies = []
        for o in range(1, n_z):
            c = pltpu.make_async_remote_copy(
                src_ref=zbuf.at[z, held(part)], dst_ref=zbuf.at[z, held(part)],
                send_sem=zssem.at[j, o], recv_sem=zrsem.at[j, o], device_id=z_peer(o), device_id_type=MESH)
            c.start()
            copies.append(c)
        along.append(copies)
    for j, part in enumerate(parts):
        for c in along[j]:
            c.wait_recv()
        total = zbuf[0, held(part)]
        for k in range(1, n_z):
            total = total + zbuf[k, held(part)]
        out_ref[mine(part, me), :] = total
        copies = []
        for o in range(1, n_p):
            c = pltpu.make_async_remote_copy(
                src_ref=out_ref.at[mine(part, me)], dst_ref=out_ref.at[mine(part, me)],
                send_sem=cssem.at[j, o], recv_sem=crsem.at[j, o], device_id=plane_peer(o)[1], device_id_type=MESH)
            c.start()
            copies.append(c)
        back.append(copies)
    for copies in sent + along:
        for c in copies:
            c.wait_send()
    for copies in back:
        for c in copies:
            c.wait()


def split_rows(share, n_p):
    first = -(-share // 16) * 8
    parts, base, off = [], 0, 0
    for rows in (first, share - first):
        if rows:
            parts.append((base, off, rows))
            base += n_p * rows
            off += rows
    return parts


def merge(left, right):
    lane = lax.broadcasted_iota(jnp.int32, left.shape, 1)
    return jnp.where(lane < HALF, pltpu.roll(left, HALF, 1), right)


def matrix_and_gram(field, time_taps, lat_kernel, lon_kernel, weights):
    rows_lat, cols, length = field.shape
    size = rows_lat * cols
    steps = length - time_taps.shape[0] + 1
    chunks = steps // LANES
    fits = [q for q in range(1, rows_lat + 1) if rows_lat % q == 0 and q * cols % 8 == 0]
    group = next((q for q in fits if q * cols >= 64), fits[-1])
    step = group * cols
    pieces = rows_lat // group
    span = -(-(LANES + time_taps.shape[0] - 1) // LANES) * LANES
    blocks = chunks * chunks + -(-chunks // 2)
    n_lat, n_lon = lax.axis_size("lat"), lax.axis_size("lon")
    pair = 2 if n_lon % 2 == 0 else 1
    n_p, n_z = n_lat * pair, n_lon // pair
    share = -(-(blocks * HALF) // (8 * n_p)) * 8
    packed = share * n_p
    parts = len(split_rows(share, n_p))
    dma = pltpu.SemaphoreType.DMA
    vmem, smem = pl.BlockSpec(memory_space=pltpu.VMEM), pl.BlockSpec(memory_space=pltpu.SMEM)
    return pl.pallas_call(
        functools.partial(front_kernel, n_lat, n_lon, pair, cols, group),
        out_shape=(jax.ShapeDtypeStruct((size, steps), jnp.float32), jax.ShapeDtypeStruct((packed, LANES), jnp.float32)),
        in_specs=[vmem, vmem, smem, smem, smem],
        out_specs=(vmem, vmem),
        scratch_shapes=[
            pltpu.VMEM((size, length), jnp.float32),
            pltpu.VMEM((1, span), jnp.float32),
            pltpu.VMEM((step, 3 * step), jnp.float32),
            pltpu.VMEM((chunks, 3 * size, LANES), jnp.float32),
            pltpu.VMEM((chunks, 3, size, LANES), jnp.float32),
            pltpu.VMEM((packed, LANES), jnp.float32),
            pltpu.VMEM((n_p, share, LANES), jnp.float32),
            pltpu.VMEM((n_z, share, LANES), jnp.float32),
        ] + [dma((chunks, pieces))] * 4 + [dma((chunks, pieces, 2))] * 2
        + [dma((parts, n_p))] * 2 + [dma((parts, n_z))] * 2 + [dma((parts, n_p))] * 2,
        compiler_params=pltpu.CompilerParams(collective_id=0, has_side_effects=True),
        name="front",
    )(field, time_taps, lat_kernel, lon_kernel, weights)


def body(field, lat_kernel, lon_kernel, time_taps):
    rows_lat, rows_lon = field.shape[:2]
    total_lat = rows_lat * lax.axis_size("lat")
    cells = total_lat * rows_lon * lax.axis_size("lon")
    latitude = np.pi * (np.arange(total_lat) + 0.5) / total_lat - np.pi / 2
    weights = jnp.asarray(np.sqrt(np.cos(latitude)), jnp.float32)
    matrix, gram = matrix_and_gram(field, time_taps, lat_kernel, lon_kernel, weights)
    upper, basis = factor(gram, matrix, float(cells) ** 0.5, rows_lat, rows_lon)
    return (basis, upper)


def solution(mesh):
    placed = (P("lat", "lon", None), P(), P(), P())
    return jax.shard_map(
        body, mesh=mesh, in_specs=placed, out_specs=(P("lat", "lon", None), P()), check_vma=False
    )
```

```python
import functools

import jax
import jax.numpy as jnp
import numpy as np
from jax import lax
from jax.experimental import pallas as pl
from jax.experimental.pallas import tpu as pltpu
from jax.sharding import PartitionSpec as P


MESH = pl.DeviceIdType.MESH
NB = 64
LANES = 128
HALF = LANES // 2


def spread(x, q):
    return jnp.broadcast_to(x[q:q + 1, :], (8, LANES))


def column(x, lane):
    return jnp.take_along_axis(x, jnp.full(x.shape, lane, jnp.int32), axis=1, mode="promise_in_bounds")


def eliminate(grp, first):
    sub = lax.broadcasted_iota(jnp.int32, (8, LANES), 0)
    tiles = range(len(grp[0]))
    for g in range(len(grp)):
        lane = first + 8 * g
        cols = [{h: column(grp[h][0], lane + q) for h in range(g, len(grp))} for q in range(8)]
        s = {(i, j): spread(cols[j][g], i) for j in range(8) for i in range(j, 8)}
        rows = [[spread(grp[g][t], q) for t in tiles] for q in range(8)]
        inv, low, pivots = [None] * 8, {}, None
        for q in range(8):
            if q % 2 == 0:
                inv[q] = pltpu.reciprocal(s[q, q])
                inv[q + 1] = s[q, q] * pltpu.reciprocal(s[q, q] * s[q + 1, q + 1] - s[q + 1, q] * s[q + 1, q])
            pivots = s[q, q] if pivots is None else jnp.where(sub == q, s[q, q], pivots)
            for i in range(q + 1, 8):
                low[i, q] = s[i, q] * inv[q]
            for j in range(q + 1, 8):
                for i in range(j, 8):
                    s[i, j] = s[i, j] - low[i, q] * s[j, q]
        for q in range(8):
            for p in range(q + 1, 8):
                for t in tiles:
                    rows[p][t] = rows[p][t] - low[p, q] * rows[q][t]
        for h in range(g + 1, len(grp)):
            for q in range(8):
                u = cols[q][h] * inv[q]
                for p in range(q + 1, 8):
                    cols[p][h] = cols[p][h] - u * s[p, q]
                for t in tiles:
                    grp[h][t] = grp[h][t] - u * rows[q][t]
        rinv = lax.rsqrt(pivots)
        for t in tiles:
            done = rows[0][t]
            for q in range(1, 8):
                done = jnp.where(sub == q, rows[q][t], done)
            grp[g][t] = done * rinv


def factor_kernel(scale, n, g_ref, m_ref, r_ref, basis_ref, a, b, y_ref, p_ref):
    at = 0
    first = column(spread(g_ref[0:8], 0), 0)[0:1, :]
    unit = 1.0 / first
    tiles = n // LANES
    tails = []
    for t in range(tiles):
        if t:
            a[t * LANES:(t + 1) * LANES, :t * LANES] = jnp.zeros((LANES, t * LANES), jnp.float32)
        for r in range(2):
            row = t * LANES + r * HALF
            for q in range(t + r, tiles):
                a[row:row + HALF, q * LANES:(q + 1) * LANES] = g_ref[at:at + HALF] * unit
                at += HALF
        tails.append(t)
        if len(tails) == 2 or t == tiles - 1:
            both = g_ref[at:at + HALF] * unit
            at += HALF
            lane = lax.broadcasted_iota(jnp.int32, both.shape, 1)
            for u in tails:
                tail = both if u % 2 or len(tails) == 1 else pltpu.roll(both, HALF, 1)
                a[u * LANES + HALF:(u + 1) * LANES, u * LANES:(u + 1) * LANES] = jnp.where(lane < HALF, 0.0, tail)
            tails = []
    root = lax.sqrt(first)[:, :1]
    to_r = root / scale
    to_y = scale / root
    rows, cols = basis_ref.shape[:2]
    down = (((0,), (0,)), ((), ()))
    flat = (((1,), (0,)), ((), ()))
    across = (((1,), (1,)), ((), ()))

    def dot(x, y, dims):
        return lax.dot_general(x, y, dims, precision=lax.Precision.HIGHEST, preferred_element_type=jnp.float32)

    square = (LANES, LANES)
    eye = (lax.broadcasted_iota(jnp.int32, square, 0) == lax.broadcasted_iota(jnp.int32, square, 1)).astype(jnp.float32)
    for t in range(tiles):
        lo, hi = t * LANES, (t + 1) * LANES
        wide = n - lo
        b[...] = eye
        for k in range(lo, hi, NB):
            live = [(a, k, q) for q in range(t, tiles)] + [(b, k - lo, 0)]
            grp = [[ref[r + 8 * h:r + 8 * h + 8, q * LANES:(q + 1) * LANES] for ref, r, q in live] for h in range(NB // 8)]
            eliminate(grp, k - lo)
            panel = jnp.concatenate([jnp.concatenate(x, axis=1) for x in grp], axis=0)
            nxt = k + NB
            if nxt < hi:
                update = dot(panel[:, nxt - lo:LANES], panel, down)
                a[nxt:hi, lo:] = a[nxt:hi, lo:] - update[:, :wide]
                b[nxt - lo:, :] = b[nxt - lo:, :] - update[:, wide:]
            row_id = lax.broadcasted_iota(jnp.int32, (NB, wide), 0) + k
            lane_id = lax.broadcasted_iota(jnp.int32, (NB, wide), 1) + lo
            if t:
                r_ref[k:nxt, :lo] = jnp.zeros((NB, lo), jnp.float32)
            r_ref[k:nxt, lo:] = jnp.where(lane_id >= row_id, panel[:, :wide] * to_r, 0.0)
            y_ref[k:nxt, :] = panel[:, wide:]
            if hi < n:
                a[k:nxt, hi:] = panel[:, LANES:wide]
        if hi < n:
            a[hi:, hi:] = a[hi:, hi:] - dot(a[lo:hi, hi:], a[lo:hi, hi:], down)
        part = dot(p_ref[:, lo:hi] if t else m_ref[:, lo:hi], y_ref[lo:hi, :], across)
        if hi < n:
            p_ref[:, hi:] = (p_ref[:, hi:] if t else m_ref[:, hi:]) - dot(part, a[lo:hi, hi:], flat)
        for i in range(rows):
            basis_ref[i, :, lo:hi] = part[i * cols:(i + 1) * cols] * to_y


def factor(gram, matrix, scale, rows, cols):
    size, n = matrix.shape
    square = jax.ShapeDtypeStruct((n, n), jnp.float32)
    vmem = pl.BlockSpec(memory_space=pltpu.VMEM)
    return pl.pallas_call(
        functools.partial(factor_kernel, scale, n),
        out_shape=(square, jax.ShapeDtypeStruct((rows, cols, n), jnp.float32)),
        in_specs=[vmem, vmem],
        out_specs=(vmem, vmem),
        scratch_shapes=[
            pltpu.VMEM((n, n), jnp.float32), pltpu.VMEM((LANES, LANES), jnp.float32),
            pltpu.VMEM((n, LANES), jnp.float32), pltpu.VMEM((size, n), jnp.float32),
        ],
        name="factor",
    )(gram, matrix)


def front_kernel(n_lat, n_lon, pair, cols, group, x_ref, v_ref, lat_ref, lon_ref, w_ref, m_ref, out_ref, flat, row_ref, band_ref, ext, lonb, g_ref, rbuf, zbuf, psend, precv, fsend, frecv, lsend, lrecv, ssem, rsem, zssem, zrsem, cssem, crsem):
    lat, lon = lax.axis_index("lat"), lax.axis_index("lon")
    n_p, n_z = n_lat * pair, n_lon // pair
    share = g_ref.shape[0] // n_p
    core, z = lax.rem(lon, pair), lon // pair
    me = lat * pair + core
    chunks, size = lonb.shape[0], lonb.shape[2]
    rows_lat = size // cols
    taps = lat_ref.shape[0]
    step = group * cols
    pieces = size // step
    odd = lax.rem(lat, 2)
    partner = lat + 1 - 2 * odd
    target = lat + 2 - 4 * odd
    source = lat - 2 + 4 * odd
    hands_on = jnp.logical_and(target >= 0, target < n_lat)
    gets = jnp.logical_and(source >= 0, source < n_lat)
    right, left = lax.rem(lon + 1, n_lon), lax.rem(lon + n_lon - 1, n_lon)
    far = 2 * size * odd
    near = 2 * size * (1 - odd)

    def plane_peer(o):
        peer = lax.rem(me + o, n_p)
        return peer, (peer // pair, z * pair + lax.rem(peer, pair))

    def z_peer(o):
        return (lat, lax.rem(z + o, n_z) * pair + core)

    barrier = pltpu.get_barrier_semaphore()
    for o in range(1, n_p):
        pl.semaphore_signal(barrier, inc=1, device_id=plane_peer(o)[1], device_id_type=MESH)
    for o in range(1, n_z):
        pl.semaphore_signal(barrier, inc=1, device_id=z_peer(o), device_id_type=MESH)
    for side_dev in (left, right):
        pl.semaphore_signal(barrier, inc=1, device_id=(lat, side_dev), device_id_type=MESH)

    def up(k):
        return k * step + odd * ((pieces - 1 - 2 * k) * step)

    def down(k):
        return (pieces - 1 - k) * step + odd * ((2 * k - pieces + 1) * step)

    def at(start):
        return pl.ds(pl.multiple_of(start, 8), step)

    def swap(c, k):
        return pltpu.make_async_remote_copy(
            src_ref=ext.at[c, at(size + up(k))], dst_ref=ext.at[c, at(far + up(k))],
            send_sem=psend.at[c, k], recv_sem=precv.at[c, k], device_id=(partner, lon), device_id_type=MESH)

    def hand(c, k):
        return pltpu.make_async_remote_copy(
            src_ref=ext.at[c, at(near + down(k))], dst_ref=ext.at[c, at(far + down(k))],
            send_sem=fsend.at[c, k], recv_sem=frecv.at[c, k], device_id=(target, lon), device_id_type=MESH)

    def side(c, k, way):
        start = up(k) if c else down(k)
        return pltpu.make_async_remote_copy(
            src_ref=lonb.at[c, 1, at(start)], dst_ref=lonb.at[c, 2 * way, at(start)],
            send_sem=lsend.at[c, k, way], recv_sem=lrecv.at[c, k, way],
            device_id=(lat, left if way else right), device_id_type=MESH)

    def relay(c, k):
        swap(c, k).wait_recv()

        @pl.when(hands_on)
        def _():
            hand(c, k).start()

    def lat_smooth(c, start):
        sums = {}
        for k in range(taps):
            place = (k + rows_lat - taps // 2) * cols
            q = place % 8
            rows = step + 8 if q else step
            value = lat_ref[k] * ext[c, pl.ds(pl.multiple_of(start + place - q, 8), rows)]
            sums[q] = sums[q] + value if q in sums else value
        return sum(v[q:q + step] for q, v in sums.items())

    def lon_smooth(c, start):
        value = jnp.concatenate([lonb[c, p, at(start)] for p in range(3)], axis=0)
        return jnp.dot(band_ref[...], value, precision=lax.Precision.HIGHEST, preferred_element_type=jnp.float32)

    def weighted(value, start):
        row = lat * rows_lat + start // cols
        place = lax.broadcasted_iota(jnp.int32, value.shape, 0)
        weight = jnp.zeros(value.shape, jnp.float32) + w_ref[row]
        for q in range(1, group):
            weight = jnp.where(place >= q * cols, w_ref[row + q], weight)
        return value * weight

    length = x_ref.shape[2]
    half = v_ref.shape[0]
    for i in range(rows_lat):
        flat[i * cols:(i + 1) * cols] = x_ref[i]
    span = row_ref.shape[1]
    lane = lax.broadcasted_iota(jnp.int32, (1, span), 1)
    row_ref[...] = jnp.zeros((1, span), jnp.float32)
    row_ref[:, :half] = v_ref[...].reshape(1, half)
    row = jnp.where(lane == half // 2, row_ref[...] + 1.0, row_ref[...])
    shifts = pltpu.roll(jnp.broadcast_to(row, (LANES, span)), 0, 1, stride=1, stride_axis=0)

    def filtered(c):
        return lax.dot_general(
            flat[:, c * LANES:c * LANES + span], shifts, (((1,), (1,)), ((), ())),
            precision=lax.Precision.HIGHEST, preferred_element_type=jnp.float32)

    ext[0, size:2 * size] = filtered(0)
    pl.semaphore_wait(barrier, n_p + n_z)
    for k in range(pieces):
        swap(0, k).start()
    lonb[1, 1] = filtered(1)
    for k in range(pieces):
        side(1, k, 0).start()
        side(1, k, 1).start()

    @pl.when(jnp.logical_not(gets))
    def _():
        for c in range(chunks):
            ext[c, pl.ds(pl.multiple_of(far, 8), size)] = jnp.zeros((size, LANES), jnp.float32)

    bands = 3
    shape = (step, bands * step)
    r, e = lax.broadcasted_iota(jnp.int32, shape, 0), lax.broadcasted_iota(jnp.int32, shape, 1)
    part = sum((e >= p * step).astype(jnp.int32) for p in range(1, bands)) + jnp.zeros(shape, jnp.int32)
    e = e - part * step
    er = sum((e >= q * cols).astype(jnp.int32) for q in range(1, group)) + jnp.zeros(shape, jnp.int32)
    rr = sum((r >= q * cols).astype(jnp.int32) for q in range(1, group)) + jnp.zeros(shape, jnp.int32)
    offset = part * cols + (e - er * cols) - (r - rr * cols) - (cols - taps // 2)
    offset = jnp.where(er == rr, offset, -1)
    band = jnp.zeros(shape, jnp.float32)
    for k in range(taps):
        band = jnp.where(offset == k, lon_ref[k], band)
    band_ref[...] = band

    def lon_first(k):
        side(1, k, 0).wait_recv()
        side(1, k, 1).wait_recv()
        ext[1, at(size + up(k))] = lon_smooth(1, up(k))
        swap(1, k).start()

    def lat_first(k):
        @pl.when(gets)
        def _():
            hand(0, k).wait_recv()

        lonb[0, 1, at(down(k))] = lat_smooth(0, down(k))
        side(0, k, 0).start()
        side(0, k, 1).start()

    def lon_last(k):
        side(0, k, 0).wait_recv()
        side(0, k, 1).wait_recv()
        m_ref[at(down(k)), :LANES] = weighted(lon_smooth(0, down(k)), down(k))

    def lat_last(k):
        @pl.when(gets)
        def _():
            hand(1, k).wait_recv()

        m_ref[at(down(k)), LANES:] = weighted(lat_smooth(1, down(k)), down(k))

    relay_0, relay_1 = functools.partial(relay, 0), functools.partial(relay, 1)
    order = [(k, relay_0, k) for k in range(pieces)]
    order += [(k + 1.5, lon_first, k) for k in range(pieces)]
    order += [(pieces - 0.8 + k, lat_first, k) for k in range(pieces)]
    order += [(pieces + 2.5 + k, relay_1, k) for k in range(pieces)]
    order += [(3 * pieces + k, lon_last, k) for k in range(pieces)]
    order += [(3 * pieces + k + 0.5, lat_last, k) for k in range(pieces)]
    for _, do, k in sorted(order, key=lambda item: item[0]):
        do(k)

    def mine(part, who):
        base, _, rows = part
        return pl.ds(pl.multiple_of(base + who * rows, 8), rows)

    def held(part):
        return pl.ds(part[1], part[2])

    def scatter(j):
        copies = []
        for o in range(1, n_p):
            peer, dev = plane_peer(o)
            c = pltpu.make_async_remote_copy(
                src_ref=g_ref.at[mine(parts[j], peer)], dst_ref=rbuf.at[o, held(parts[j])],
                send_sem=ssem.at[j, o], recv_sem=rsem.at[j, o], device_id=dev, device_id_type=MESH)
            c.start()
            copies.append(c)
        return copies

    parts = split_rows(share, n_p)
    sent = []
    place = 0
    tails = []
    for t in range(chunks):
        both = lax.dot_general(
            m_ref[:, t * LANES:(t + 1) * LANES], m_ref[:, t * LANES:], (((0,), (0,)), ((), ())),
            precision=lax.Precision.HIGHEST, preferred_element_type=jnp.float32)
        for r in range(2):
            for q in range(r, chunks - t):
                g_ref[place:place + HALF] = both[r * HALF:(r + 1) * HALF, q * LANES:(q + 1) * LANES]
                place += HALF
        tails.append(both[HALF:, :LANES])
        if len(tails) == 2 or t == chunks - 1:
            g_ref[place:place + HALF] = merge(tails[0], tails[-1])
            place += HALF
            tails = []
        if t == chunks - 1 and place < g_ref.shape[0]:
            g_ref[place:] = jnp.zeros((g_ref.shape[0] - place, LANES), jnp.float32)
            place = g_ref.shape[0]
        while len(sent) < len(parts) and parts[len(sent)][0] + n_p * parts[len(sent)][2] <= place:
            sent.append(scatter(len(sent)))

    for c in range(chunks):
        for k in range(pieces):
            swap(c, k).wait_send()
            side(c, k, 0).wait_send()
            side(c, k, 1).wait_send()

    @pl.when(hands_on)
    def _():
        for c in range(chunks):
            for k in range(pieces):
                hand(c, k).wait_send()

    along, back = [], []
    for j, part in enumerate(parts):
        acc = g_ref[mine(part, me), :]
        for o in range(1, n_p):
            sent[j][o - 1].wait_recv()
            acc = acc + rbuf[o, held(part)]
        zbuf[z, held(part)] = acc
        copies = []
        for o in range(1, n_z):
            c = pltpu.make_async_remote_copy(
                src_ref=zbuf.at[z, held(part)], dst_ref=zbuf.at[z, held(part)],
                send_sem=zssem.at[j, o], recv_sem=zrsem.at[j, o], device_id=z_peer(o), device_id_type=MESH)
            c.start()
            copies.append(c)
        along.append(copies)
    for j, part in enumerate(parts):
        for c in along[j]:
            c.wait_recv()
        total = zbuf[0, held(part)]
        for k in range(1, n_z):
            total = total + zbuf[k, held(part)]
        out_ref[mine(part, me), :] = total
        copies = []
        for o in range(1, n_p):
            c = pltpu.make_async_remote_copy(
                src_ref=out_ref.at[mine(part, me)], dst_ref=out_ref.at[mine(part, me)],
                send_sem=cssem.at[j, o], recv_sem=crsem.at[j, o], device_id=plane_peer(o)[1], device_id_type=MESH)
            c.start()
            copies.append(c)
        back.append(copies)
    for copies in sent + along:
        for c in copies:
            c.wait_send()
    for copies in back:
        for c in copies:
            c.wait()


def split_rows(share, n_p):
    first = -(-share // 16) * 8
    parts, base, off = [], 0, 0
    for rows in (first, share - first):
        if rows:
            parts.append((base, off, rows))
            base += n_p * rows
            off += rows
    return parts


def merge(left, right):
    lane = lax.broadcasted_iota(jnp.int32, left.shape, 1)
    return jnp.where(lane < HALF, pltpu.roll(left, HALF, 1), right)


def matrix_and_gram(field, time_taps, lat_kernel, lon_kernel, weights):
    rows_lat, cols, length = field.shape
    size = rows_lat * cols
    steps = length - time_taps.shape[0] + 1
    chunks = steps // LANES
    fits = [q for q in range(1, rows_lat + 1) if rows_lat % q == 0 and q * cols % 8 == 0]
    group = next((q for q in fits if q * cols >= 64), fits[-1])
    step = group * cols
    pieces = rows_lat // group
    span = -(-(LANES + time_taps.shape[0] - 1) // LANES) * LANES
    blocks = chunks * chunks + -(-chunks // 2)
    n_lat, n_lon = lax.axis_size("lat"), lax.axis_size("lon")
    pair = 2 if n_lon % 2 == 0 else 1
    n_p, n_z = n_lat * pair, n_lon // pair
    share = -(-(blocks * HALF) // (8 * n_p)) * 8
    packed = share * n_p
    parts = len(split_rows(share, n_p))
    dma = pltpu.SemaphoreType.DMA
    vmem, smem = pl.BlockSpec(memory_space=pltpu.VMEM), pl.BlockSpec(memory_space=pltpu.SMEM)
    return pl.pallas_call(
        functools.partial(front_kernel, n_lat, n_lon, pair, cols, group),
        out_shape=(jax.ShapeDtypeStruct((size, steps), jnp.float32), jax.ShapeDtypeStruct((packed, LANES), jnp.float32)),
        in_specs=[vmem, vmem, smem, smem, smem],
        out_specs=(vmem, vmem),
        scratch_shapes=[
            pltpu.VMEM((size, length), jnp.float32),
            pltpu.VMEM((1, span), jnp.float32),
            pltpu.VMEM((step, 3 * step), jnp.float32),
            pltpu.VMEM((chunks, 3 * size, LANES), jnp.float32),
            pltpu.VMEM((chunks, 3, size, LANES), jnp.float32),
            pltpu.VMEM((packed, LANES), jnp.float32),
            pltpu.VMEM((n_p, share, LANES), jnp.float32),
            pltpu.VMEM((n_z, share, LANES), jnp.float32),
        ] + [dma((chunks, pieces))] * 4 + [dma((chunks, pieces, 2))] * 2
        + [dma((parts, n_p))] * 2 + [dma((parts, n_z))] * 2 + [dma((parts, n_p))] * 2,
        compiler_params=pltpu.CompilerParams(collective_id=0, has_side_effects=True),
        name="front",
    )(field, time_taps, lat_kernel, lon_kernel, weights)


def body(field, lat_kernel, lon_kernel, time_taps):
    rows_lat, rows_lon = field.shape[:2]
    total_lat = rows_lat * lax.axis_size("lat")
    cells = total_lat * rows_lon * lax.axis_size("lon")
    latitude = np.pi * (np.arange(total_lat) + 0.5) / total_lat - np.pi / 2
    weights = jnp.asarray(np.sqrt(np.cos(latitude)), jnp.float32)
    matrix, gram = matrix_and_gram(field, time_taps, lat_kernel, lon_kernel, weights)
    upper, basis = factor(gram, matrix, float(cells) ** 0.5, rows_lat, rows_lon)
    return (basis, upper)


def solution(mesh):
    placed = (P("lat", "lon", None), P(), P(), P())
    return jax.shard_map(
        body, mesh=mesh, in_specs=placed, out_specs=(P("lat", "lon", None), P()), check_vma=False
    )
```

```python
import functools

import jax
import jax.numpy as jnp
import numpy as np
from jax import lax
from jax.experimental import pallas as pl
from jax.experimental.pallas import tpu as pltpu
from jax.sharding import PartitionSpec as P


MESH = pl.DeviceIdType.MESH
NB = 64
LANES = 128
HALF = LANES // 2


def spread(x, q):
    return jnp.broadcast_to(x[q:q + 1, :], (8, LANES))


def column(x, lane):
    return jnp.take_along_axis(x, jnp.full(x.shape, lane, jnp.int32), axis=1, mode="promise_in_bounds")


def eliminate(grp, first):
    sub = lax.broadcasted_iota(jnp.int32, (8, LANES), 0)
    tiles = range(len(grp[0]))
    for g in range(len(grp)):
        lane = first + 8 * g
        cols = [{h: column(grp[h][0], lane + q) for h in range(g, len(grp))} for q in range(8)]
        s = {(i, j): spread(cols[j][g], i) for j in range(8) for i in range(j, 8)}
        rows = [[spread(grp[g][t], q) for t in tiles] for q in range(8)]
        inv, low, pivots = [None] * 8, {}, None
        for q in range(8):
            if q % 2 == 0:
                inv[q] = pltpu.reciprocal(s[q, q])
                inv[q + 1] = s[q, q] * pltpu.reciprocal(s[q, q] * s[q + 1, q + 1] - s[q + 1, q] * s[q + 1, q])
            pivots = s[q, q] if pivots is None else jnp.where(sub == q, s[q, q], pivots)
            for i in range(q + 1, 8):
                low[i, q] = s[i, q] * inv[q]
            for j in range(q + 1, 8):
                for i in range(j, 8):
                    s[i, j] = s[i, j] - low[i, q] * s[j, q]
        for q in range(8):
            for p in range(q + 1, 8):
                for t in tiles:
                    rows[p][t] = rows[p][t] - low[p, q] * rows[q][t]
        for h in range(g + 1, len(grp)):
            for q in range(8):
                u = cols[q][h] * inv[q]
                for p in range(q + 1, 8):
                    cols[p][h] = cols[p][h] - u * s[p, q]
                for t in tiles:
                    grp[h][t] = grp[h][t] - u * rows[q][t]
        rinv = lax.rsqrt(pivots)
        for t in tiles:
            done = rows[0][t]
            for q in range(1, 8):
                done = jnp.where(sub == q, rows[q][t], done)
            grp[g][t] = done * rinv


def factor_kernel(scale, n, g_ref, m_hbm, r_hbm, basis_hbm, m_ref, r_ref, basis_ref, a, b, y_ref, p_ref, m_sem, r_sem, basis_sem):
    fetch = pltpu.make_async_copy(m_hbm, m_ref, m_sem)
    fetch.start()
    stores = []
    at = 0
    first = column(spread(g_ref[0:8], 0), 0)[0:1, :]
    unit = 1.0 / first
    tiles = n // LANES
    tails = []
    for t in range(tiles):
        if t:
            a[t * LANES:(t + 1) * LANES, :t * LANES] = jnp.zeros((LANES, t * LANES), jnp.float32)
        for r in range(2):
            row = t * LANES + r * HALF
            for q in range(t + r, tiles):
                a[row:row + HALF, q * LANES:(q + 1) * LANES] = g_ref[at:at + HALF] * unit
                at += HALF
        tails.append(t)
        if len(tails) == 2 or t == tiles - 1:
            both = g_ref[at:at + HALF] * unit
            at += HALF
            lane = lax.broadcasted_iota(jnp.int32, both.shape, 1)
            for u in tails:
                tail = both if u % 2 or len(tails) == 1 else pltpu.roll(both, HALF, 1)
                a[u * LANES + HALF:(u + 1) * LANES, u * LANES:(u + 1) * LANES] = jnp.where(lane < HALF, 0.0, tail)
            tails = []
    root = lax.sqrt(first)[:, :1]
    to_r = root / scale
    to_y = scale / root
    rows, cols = basis_hbm.shape[:2]
    down = (((0,), (0,)), ((), ()))
    flat = (((1,), (0,)), ((), ()))
    across = (((1,), (1,)), ((), ()))

    def dot(x, y, dims):
        return lax.dot_general(x, y, dims, precision=lax.Precision.HIGHEST, preferred_element_type=jnp.float32)

    square = (LANES, LANES)
    eye = (lax.broadcasted_iota(jnp.int32, square, 0) == lax.broadcasted_iota(jnp.int32, square, 1)).astype(jnp.float32)
    for t in range(tiles):
        lo, hi = t * LANES, (t + 1) * LANES
        wide = n - lo
        b[...] = eye
        for k in range(lo, hi, NB):
            live = [(a, k, q) for q in range(t, tiles)] + [(b, k - lo, 0)]
            grp = [[ref[r + 8 * h:r + 8 * h + 8, q * LANES:(q + 1) * LANES] for ref, r, q in live] for h in range(NB // 8)]
            eliminate(grp, k - lo)
            panel = jnp.concatenate([jnp.concatenate(x, axis=1) for x in grp], axis=0)
            nxt = k + NB
            if nxt < hi:
                update = dot(panel[:, nxt - lo:LANES], panel, down)
                a[nxt:hi, lo:] = a[nxt:hi, lo:] - update[:, :wide]
                b[nxt - lo:, :] = b[nxt - lo:, :] - update[:, wide:]
            row_id = lax.broadcasted_iota(jnp.int32, (NB, wide), 0) + k
            lane_id = lax.broadcasted_iota(jnp.int32, (NB, wide), 1) + lo
            if t:
                r_ref[k:nxt, :lo] = jnp.zeros((NB, lo), jnp.float32)
            r_ref[k:nxt, lo:] = jnp.where(lane_id >= row_id, panel[:, :wide] * to_r, 0.0)
            y_ref[k:nxt, :] = panel[:, wide:]
            if hi < n:
                a[k:nxt, hi:] = panel[:, LANES:wide]
        if hi < n:
            a[hi:, hi:] = a[hi:, hi:] - dot(a[lo:hi, hi:], a[lo:hi, hi:], down)
        if t == 0:
            fetch.wait()
        stores.append(pltpu.make_async_copy(r_ref.at[lo:hi], r_hbm.at[lo:hi], r_sem.at[t]))
        stores[-1].start()
        part = dot(p_ref[:, lo:hi] if t else m_ref[:, lo:hi], y_ref[lo:hi, :], across)
        if hi < n:
            p_ref[:, hi:] = (p_ref[:, hi:] if t else m_ref[:, hi:]) - dot(part, a[lo:hi, hi:], flat)
        for i in range(rows):
            basis_ref[i, :, lo:hi] = part[i * cols:(i + 1) * cols] * to_y
        stores.append(pltpu.make_async_copy(basis_ref.at[:, :, lo:hi], basis_hbm.at[:, :, lo:hi], basis_sem.at[t]))
        stores[-1].start()
    for store in stores:
        store.wait()


def factor(gram, matrix, scale, rows, cols):
    size, n = matrix.shape
    square = jax.ShapeDtypeStruct((n, n), jnp.float32)
    vmem = pl.BlockSpec(memory_space=pltpu.VMEM)
    return pl.pallas_call(
        functools.partial(factor_kernel, scale, n),
        out_shape=(square, jax.ShapeDtypeStruct((rows, cols, n), jnp.float32)),
        in_specs=[vmem, pl.BlockSpec(memory_space=pl.ANY)],
        out_specs=(pl.BlockSpec(memory_space=pl.ANY),) * 2,
        scratch_shapes=[
            pltpu.VMEM((size, n), jnp.float32), pltpu.VMEM((n, n), jnp.float32), pltpu.VMEM((rows, cols, n), jnp.float32),
            pltpu.VMEM((n, n), jnp.float32), pltpu.VMEM((LANES, LANES), jnp.float32),
            pltpu.VMEM((n, LANES), jnp.float32), pltpu.VMEM((size, n), jnp.float32),
            pltpu.SemaphoreType.DMA, pltpu.SemaphoreType.DMA((n // LANES,)), pltpu.SemaphoreType.DMA((n // LANES,)),
        ],
        name="factor",
    )(gram, matrix)


def front_kernel(n_lat, n_lon, pair, cols, group, x_ref, v_ref, lat_ref, lon_ref, w_ref, m_hbm, out_ref, m_ref, m_sem, flat, row_ref, band_ref, ext, lonb, g_ref, rbuf, zbuf, psend, precv, fsend, frecv, lsend, lrecv, ssem, rsem, zssem, zrsem, cssem, crsem):
    lat, lon = lax.axis_index("lat"), lax.axis_index("lon")
    n_p, n_z = n_lat * pair, n_lon // pair
    share = g_ref.shape[0] // n_p
    core, z = lax.rem(lon, pair), lon // pair
    me = lat * pair + core
    chunks, size = lonb.shape[0], lonb.shape[2]
    rows_lat = size // cols
    taps = lat_ref.shape[0]
    step = group * cols
    pieces = size // step
    odd = lax.rem(lat, 2)
    partner = lat + 1 - 2 * odd
    target = lat + 2 - 4 * odd
    source = lat - 2 + 4 * odd
    hands_on = jnp.logical_and(target >= 0, target < n_lat)
    gets = jnp.logical_and(source >= 0, source < n_lat)
    right, left = lax.rem(lon + 1, n_lon), lax.rem(lon + n_lon - 1, n_lon)
    far = 2 * size * odd
    near = 2 * size * (1 - odd)

    def plane_peer(o):
        peer = lax.rem(me + o, n_p)
        return peer, (peer // pair, z * pair + lax.rem(peer, pair))

    def z_peer(o):
        return (lat, lax.rem(z + o, n_z) * pair + core)

    barrier = pltpu.get_barrier_semaphore()
    for o in range(1, n_p):
        pl.semaphore_signal(barrier, inc=1, device_id=plane_peer(o)[1], device_id_type=MESH)
    for o in range(1, n_z):
        pl.semaphore_signal(barrier, inc=1, device_id=z_peer(o), device_id_type=MESH)
    for side_dev in (left, right):
        pl.semaphore_signal(barrier, inc=1, device_id=(lat, side_dev), device_id_type=MESH)

    def up(k):
        return k * step + odd * ((pieces - 1 - 2 * k) * step)

    def down(k):
        return (pieces - 1 - k) * step + odd * ((2 * k - pieces + 1) * step)

    def at(start):
        return pl.ds(pl.multiple_of(start, 8), step)

    def swap(c, k):
        return pltpu.make_async_remote_copy(
            src_ref=ext.at[c, at(size + up(k))], dst_ref=ext.at[c, at(far + up(k))],
            send_sem=psend.at[c, k], recv_sem=precv.at[c, k], device_id=(partner, lon), device_id_type=MESH)

    def hand(c, k):
        return pltpu.make_async_remote_copy(
            src_ref=ext.at[c, at(near + down(k))], dst_ref=ext.at[c, at(far + down(k))],
            send_sem=fsend.at[c, k], recv_sem=frecv.at[c, k], device_id=(target, lon), device_id_type=MESH)

    def side(c, k, way):
        start = up(k) if c else down(k)
        return pltpu.make_async_remote_copy(
            src_ref=lonb.at[c, 1, at(start)], dst_ref=lonb.at[c, 2 * way, at(start)],
            send_sem=lsend.at[c, k, way], recv_sem=lrecv.at[c, k, way],
            device_id=(lat, left if way else right), device_id_type=MESH)

    def relay(c, k):
        swap(c, k).wait_recv()

        @pl.when(hands_on)
        def _():
            hand(c, k).start()

    def lat_smooth(c, start):
        sums = {}
        for k in range(taps):
            place = (k + rows_lat - taps // 2) * cols
            q = place % 8
            rows = step + 8 if q else step
            value = lat_ref[k] * ext[c, pl.ds(pl.multiple_of(start + place - q, 8), rows)]
            sums[q] = sums[q] + value if q in sums else value
        return sum(v[q:q + step] for q, v in sums.items())

    def lon_smooth(c, start):
        value = jnp.concatenate([lonb[c, p, at(start)] for p in range(3)], axis=0)
        return jnp.dot(band_ref[...], value, precision=lax.Precision.HIGHEST, preferred_element_type=jnp.float32)

    def weighted(value, start):
        row = lat * rows_lat + start // cols
        place = lax.broadcasted_iota(jnp.int32, value.shape, 0)
        weight = jnp.zeros(value.shape, jnp.float32) + w_ref[row]
        for q in range(1, group):
            weight = jnp.where(place >= q * cols, w_ref[row + q], weight)
        return value * weight

    length = x_ref.shape[2]
    half = v_ref.shape[0]
    for i in range(rows_lat):
        flat[i * cols:(i + 1) * cols] = x_ref[i]
    span = row_ref.shape[1]
    lane = lax.broadcasted_iota(jnp.int32, (1, span), 1)
    row_ref[...] = jnp.zeros((1, span), jnp.float32)
    row_ref[:, :half] = v_ref[...].reshape(1, half)
    row = jnp.where(lane == half // 2, row_ref[...] + 1.0, row_ref[...])
    shifts = pltpu.roll(jnp.broadcast_to(row, (LANES, span)), 0, 1, stride=1, stride_axis=0)

    def filtered(c):
        return lax.dot_general(
            flat[:, c * LANES:c * LANES + span], shifts, (((1,), (1,)), ((), ())),
            precision=lax.Precision.HIGHEST, preferred_element_type=jnp.float32)

    ext[0, size:2 * size] = filtered(0)
    pl.semaphore_wait(barrier, n_p + n_z)
    for k in range(pieces):
        swap(0, k).start()
    lonb[1, 1] = filtered(1)
    for k in range(pieces):
        side(1, k, 0).start()
        side(1, k, 1).start()

    @pl.when(jnp.logical_not(gets))
    def _():
        for c in range(chunks):
            ext[c, pl.ds(pl.multiple_of(far, 8), size)] = jnp.zeros((size, LANES), jnp.float32)

    bands = 3
    shape = (step, bands * step)
    r, e = lax.broadcasted_iota(jnp.int32, shape, 0), lax.broadcasted_iota(jnp.int32, shape, 1)
    part = sum((e >= p * step).astype(jnp.int32) for p in range(1, bands)) + jnp.zeros(shape, jnp.int32)
    e = e - part * step
    er = sum((e >= q * cols).astype(jnp.int32) for q in range(1, group)) + jnp.zeros(shape, jnp.int32)
    rr = sum((r >= q * cols).astype(jnp.int32) for q in range(1, group)) + jnp.zeros(shape, jnp.int32)
    offset = part * cols + (e - er * cols) - (r - rr * cols) - (cols - taps // 2)
    offset = jnp.where(er == rr, offset, -1)
    band = jnp.zeros(shape, jnp.float32)
    for k in range(taps):
        band = jnp.where(offset == k, lon_ref[k], band)
    band_ref[...] = band

    def lon_first(k):
        side(1, k, 0).wait_recv()
        side(1, k, 1).wait_recv()
        ext[1, at(size + up(k))] = lon_smooth(1, up(k))
        swap(1, k).start()

    def lat_first(k):
        @pl.when(gets)
        def _():
            hand(0, k).wait_recv()

        lonb[0, 1, at(down(k))] = lat_smooth(0, down(k))
        side(0, k, 0).start()
        side(0, k, 1).start()

    def lon_last(k):
        side(0, k, 0).wait_recv()
        side(0, k, 1).wait_recv()
        m_ref[at(down(k)), :LANES] = weighted(lon_smooth(0, down(k)), down(k))

    def lat_last(k):
        @pl.when(gets)
        def _():
            hand(1, k).wait_recv()

        m_ref[at(down(k)), LANES:] = weighted(lat_smooth(1, down(k)), down(k))

    relay_0, relay_1 = functools.partial(relay, 0), functools.partial(relay, 1)
    order = [(k, relay_0, k) for k in range(pieces)]
    order += [(k + 1.5, lon_first, k) for k in range(pieces)]
    order += [(pieces - 0.8 + k, lat_first, k) for k in range(pieces)]
    order += [(pieces + 2.5 + k, relay_1, k) for k in range(pieces)]
    order += [(3 * pieces + k, lon_last, k) for k in range(pieces)]
    order += [(3 * pieces + k + 0.5, lat_last, k) for k in range(pieces)]
    for _, do, k in sorted(order, key=lambda item: item[0]):
        do(k)

    def mine(part, who):
        base, _, rows = part
        return pl.ds(pl.multiple_of(base + who * rows, 8), rows)

    def held(part):
        return pl.ds(part[1], part[2])

    def scatter(j):
        copies = []
        for o in range(1, n_p):
            peer, dev = plane_peer(o)
            c = pltpu.make_async_remote_copy(
                src_ref=g_ref.at[mine(parts[j], peer)], dst_ref=rbuf.at[o, held(parts[j])],
                send_sem=ssem.at[j, o], recv_sem=rsem.at[j, o], device_id=dev, device_id_type=MESH)
            c.start()
            copies.append(c)
        return copies

    keep = pltpu.make_async_copy(m_ref, m_hbm, m_sem)
    keep.start()
    parts = split_rows(share, n_p)
    sent = []
    place = 0
    tails = []
    for t in range(chunks):
        both = lax.dot_general(
            m_ref[:, t * LANES:(t + 1) * LANES], m_ref[:, t * LANES:], (((0,), (0,)), ((), ())),
            precision=lax.Precision.HIGHEST, preferred_element_type=jnp.float32)
        for r in range(2):
            for q in range(r, chunks - t):
                g_ref[place:place + HALF] = both[r * HALF:(r + 1) * HALF, q * LANES:(q + 1) * LANES]
                place += HALF
        tails.append(both[HALF:, :LANES])
        if len(tails) == 2 or t == chunks - 1:
            g_ref[place:place + HALF] = merge(tails[0], tails[-1])
            place += HALF
            tails = []
        if t == chunks - 1 and place < g_ref.shape[0]:
            g_ref[place:] = jnp.zeros((g_ref.shape[0] - place, LANES), jnp.float32)
            place = g_ref.shape[0]
        while len(sent) < len(parts) and parts[len(sent)][0] + n_p * parts[len(sent)][2] <= place:
            sent.append(scatter(len(sent)))

    for c in range(chunks):
        for k in range(pieces):
            swap(c, k).wait_send()
            side(c, k, 0).wait_send()
            side(c, k, 1).wait_send()

    @pl.when(hands_on)
    def _():
        for c in range(chunks):
            for k in range(pieces):
                hand(c, k).wait_send()

    along, back = [], []
    for j, part in enumerate(parts):
        acc = g_ref[mine(part, me), :]
        for o in range(1, n_p):
            sent[j][o - 1].wait_recv()
            acc = acc + rbuf[o, held(part)]
        zbuf[z, held(part)] = acc
        copies = []
        for o in range(1, n_z):
            c = pltpu.make_async_remote_copy(
                src_ref=zbuf.at[z, held(part)], dst_ref=zbuf.at[z, held(part)],
                send_sem=zssem.at[j, o], recv_sem=zrsem.at[j, o], device_id=z_peer(o), device_id_type=MESH)
            c.start()
            copies.append(c)
        along.append(copies)
    for j, part in enumerate(parts):
        for c in along[j]:
            c.wait_recv()
        total = zbuf[0, held(part)]
        for k in range(1, n_z):
            total = total + zbuf[k, held(part)]
        out_ref[mine(part, me), :] = total
        copies = []
        for o in range(1, n_p):
            c = pltpu.make_async_remote_copy(
                src_ref=out_ref.at[mine(part, me)], dst_ref=out_ref.at[mine(part, me)],
                send_sem=cssem.at[j, o], recv_sem=crsem.at[j, o], device_id=plane_peer(o)[1], device_id_type=MESH)
            c.start()
            copies.append(c)
        back.append(copies)
    for copies in sent + along:
        for c in copies:
            c.wait_send()
    keep.wait()
    for copies in back:
        for c in copies:
            c.wait()


def split_rows(share, n_p):
    first = share
    parts, base, off = [], 0, 0
    for rows in (first, share - first):
        if rows:
            parts.append((base, off, rows))
            base += n_p * rows
            off += rows
    return parts


def merge(left, right):
    lane = lax.broadcasted_iota(jnp.int32, left.shape, 1)
    return jnp.where(lane < HALF, pltpu.roll(left, HALF, 1), right)


def matrix_and_gram(field, time_taps, lat_kernel, lon_kernel, weights):
    rows_lat, cols, length = field.shape
    size = rows_lat * cols
    steps = length - time_taps.shape[0] + 1
    chunks = steps // LANES
    fits = [q for q in range(1, rows_lat + 1) if rows_lat % q == 0 and q * cols % 8 == 0]
    group = next((q for q in fits if q * cols >= 64), fits[-1])
    step = group * cols
    pieces = rows_lat // group
    span = -(-(LANES + time_taps.shape[0] - 1) // LANES) * LANES
    blocks = chunks * chunks + -(-chunks // 2)
    n_lat, n_lon = lax.axis_size("lat"), lax.axis_size("lon")
    pair = 2 if n_lon % 2 == 0 else 1
    n_p, n_z = n_lat * pair, n_lon // pair
    share = -(-(blocks * HALF) // (8 * n_p)) * 8
    packed = share * n_p
    parts = len(split_rows(share, n_p))
    dma = pltpu.SemaphoreType.DMA
    vmem, smem = pl.BlockSpec(memory_space=pltpu.VMEM), pl.BlockSpec(memory_space=pltpu.SMEM)
    return pl.pallas_call(
        functools.partial(front_kernel, n_lat, n_lon, pair, cols, group),
        out_shape=(jax.ShapeDtypeStruct((size, steps), jnp.float32), jax.ShapeDtypeStruct((packed, LANES), jnp.float32)),
        in_specs=[vmem, vmem, smem, smem, smem],
        out_specs=(pl.BlockSpec(memory_space=pl.ANY), vmem),
        scratch_shapes=[
            pltpu.VMEM((size, steps), jnp.float32),
            dma,
            pltpu.VMEM((size, length), jnp.float32),
            pltpu.VMEM((1, span), jnp.float32),
            pltpu.VMEM((step, 3 * step), jnp.float32),
            pltpu.VMEM((chunks, 3 * size, LANES), jnp.float32),
            pltpu.VMEM((chunks, 3, size, LANES), jnp.float32),
            pltpu.VMEM((packed, LANES), jnp.float32),
            pltpu.VMEM((n_p, share, LANES), jnp.float32),
            pltpu.VMEM((n_z, share, LANES), jnp.float32),
        ] + [dma((chunks, pieces))] * 4 + [dma((chunks, pieces, 2))] * 2
        + [dma((parts, n_p))] * 2 + [dma((parts, n_z))] * 2 + [dma((parts, n_p))] * 2,
        compiler_params=pltpu.CompilerParams(collective_id=0, has_side_effects=True),
        name="front",
    )(field, time_taps, lat_kernel, lon_kernel, weights)


def body(field, lat_kernel, lon_kernel, time_taps):
    rows_lat, rows_lon = field.shape[:2]
    total_lat = rows_lat * lax.axis_size("lat")
    cells = total_lat * rows_lon * lax.axis_size("lon")
    latitude = np.pi * (np.arange(total_lat) + 0.5) / total_lat - np.pi / 2
    weights = jnp.asarray(np.sqrt(np.cos(latitude)), jnp.float32)
    matrix, gram = matrix_and_gram(field, time_taps, lat_kernel, lon_kernel, weights)
    upper, basis = factor(gram, matrix, float(cells) ** 0.5, rows_lat, rows_lon)
    return (basis, upper)


def solution(mesh):
    placed = (P("lat", "lon", None), P(), P(), P())
    return jax.shard_map(
        body, mesh=mesh, in_specs=placed, out_specs=(P("lat", "lon", None), P()), check_vma=False
    )
```

```python
import functools

import jax
import jax.numpy as jnp
import numpy as np
from jax import lax
from jax.experimental import pallas as pl
from jax.experimental.pallas import tpu as pltpu
from jax.sharding import PartitionSpec as P


MESH = pl.DeviceIdType.MESH
NB = 64
LANES = 128
HALF = LANES // 2


def spread(x, q):
    return jnp.broadcast_to(x[q:q + 1, :], (8, LANES))


def column(x, lane):
    return jnp.take_along_axis(x, jnp.full(x.shape, lane, jnp.int32), axis=1, mode="promise_in_bounds")


def eliminate(grp, first):
    sub = lax.broadcasted_iota(jnp.int32, (8, LANES), 0)
    tiles = range(len(grp[0]))
    for g in range(len(grp)):
        lane = first + 8 * g
        cols = [{h: column(grp[h][0], lane + q) for h in range(g, len(grp))} for q in range(8)]
        s = {(i, j): spread(cols[j][g], i) for j in range(8) for i in range(j, 8)}
        rows = [[spread(grp[g][t], q) for t in tiles] for q in range(8)]
        inv, low, pivots = [None] * 8, {}, None
        for q in range(8):
            if q % 2 == 0:
                inv[q] = pltpu.reciprocal(s[q, q])
                inv[q + 1] = s[q, q] * pltpu.reciprocal(s[q, q] * s[q + 1, q + 1] - s[q + 1, q] * s[q + 1, q])
            pivots = s[q, q] if pivots is None else jnp.where(sub == q, s[q, q], pivots)
            for i in range(q + 1, 8):
                low[i, q] = s[i, q] * inv[q]
            for j in range(q + 1, 8):
                for i in range(j, 8):
                    s[i, j] = s[i, j] - low[i, q] * s[j, q]
        for q in range(8):
            for p in range(q + 1, 8):
                for t in tiles:
                    rows[p][t] = rows[p][t] - low[p, q] * rows[q][t]
        for h in range(g + 1, len(grp)):
            for q in range(8):
                u = cols[q][h] * inv[q]
                for p in range(q + 1, 8):
                    cols[p][h] = cols[p][h] - u * s[p, q]
                for t in tiles:
                    grp[h][t] = grp[h][t] - u * rows[q][t]
        rinv = lax.rsqrt(pivots)
        for t in tiles:
            done = rows[0][t]
            for q in range(1, 8):
                done = jnp.where(sub == q, rows[q][t], done)
            grp[g][t] = done * rinv


def factor_kernel(scale, n, g_ref, m_hbm, r_hbm, basis_hbm, m_ref, r_ref, basis_ref, a, b, y_ref, p_ref, m_sem, r_sem, basis_sem):
    fetch = pltpu.make_async_copy(m_hbm, m_ref, m_sem)
    fetch.start()
    stores = []
    at = 0
    first = column(spread(g_ref[0:8], 0), 0)[0:1, :]
    unit = 1.0 / first
    tiles = n // LANES
    tails = []
    for t in range(tiles):
        if t:
            a[t * LANES:(t + 1) * LANES, :t * LANES] = jnp.zeros((LANES, t * LANES), jnp.float32)
        for r in range(2):
            row = t * LANES + r * HALF
            for q in range(t + r, tiles):
                a[row:row + HALF, q * LANES:(q + 1) * LANES] = g_ref[at:at + HALF] * unit
                at += HALF
        tails.append(t)
        if len(tails) == 2 or t == tiles - 1:
            both = g_ref[at:at + HALF] * unit
            at += HALF
            lane = lax.broadcasted_iota(jnp.int32, both.shape, 1)
            for u in tails:
                tail = both if u % 2 or len(tails) == 1 else pltpu.roll(both, HALF, 1)
                a[u * LANES + HALF:(u + 1) * LANES, u * LANES:(u + 1) * LANES] = jnp.where(lane < HALF, 0.0, tail)
            tails = []
    root = lax.sqrt(first)[:, :1]
    to_r = root / scale
    to_y = scale / root
    rows, cols = basis_hbm.shape[:2]
    down = (((0,), (0,)), ((), ()))
    flat = (((1,), (0,)), ((), ()))
    across = (((1,), (1,)), ((), ()))

    def dot(x, y, dims):
        return lax.dot_general(x, y, dims, precision=lax.Precision.HIGHEST, preferred_element_type=jnp.float32)

    square = (LANES, LANES)
    eye = (lax.broadcasted_iota(jnp.int32, square, 0) == lax.broadcasted_iota(jnp.int32, square, 1)).astype(jnp.float32)
    for t in range(tiles):
        lo, hi = t * LANES, (t + 1) * LANES
        wide = n - lo
        b[...] = eye
        for k in range(lo, hi, NB):
            live = [(a, k, q) for q in range(t, tiles)] + [(b, k - lo, 0)]
            grp = [[ref[r + 8 * h:r + 8 * h + 8, q * LANES:(q + 1) * LANES] for ref, r, q in live] for h in range(NB // 8)]
            eliminate(grp, k - lo)
            panel = jnp.concatenate([jnp.concatenate(x, axis=1) for x in grp], axis=0)
            nxt = k + NB
            if nxt < hi:
                update = dot(panel[:, nxt - lo:LANES], panel, down)
                a[nxt:hi, lo:] = a[nxt:hi, lo:] - update[:, :wide]
                b[nxt - lo:, :] = b[nxt - lo:, :] - update[:, wide:]
            row_id = lax.broadcasted_iota(jnp.int32, (NB, wide), 0) + k
            lane_id = lax.broadcasted_iota(jnp.int32, (NB, wide), 1) + lo
            if t:
                r_ref[k:nxt, :lo] = jnp.zeros((NB, lo), jnp.float32)
            r_ref[k:nxt, lo:] = jnp.where(lane_id >= row_id, panel[:, :wide] * to_r, 0.0)
            y_ref[k:nxt, :] = panel[:, wide:]
            if hi < n:
                a[k:nxt, hi:] = panel[:, LANES:wide]
        if hi < n:
            a[hi:, hi:] = a[hi:, hi:] - dot(a[lo:hi, hi:], a[lo:hi, hi:], down)
        if t == 0:
            fetch.wait()
        stores.append(pltpu.make_async_copy(r_ref.at[lo:hi], r_hbm.at[lo:hi], r_sem.at[t]))
        stores[-1].start()
        part = dot(p_ref[:, lo:hi] if t else m_ref[:, lo:hi], y_ref[lo:hi, :], across)
        if hi < n:
            p_ref[:, hi:] = (p_ref[:, hi:] if t else m_ref[:, hi:]) - dot(part, a[lo:hi, hi:], flat)
        for i in range(rows):
            basis_ref[i, :, lo:hi] = part[i * cols:(i + 1) * cols] * to_y
        stores.append(pltpu.make_async_copy(basis_ref.at[:, :, lo:hi], basis_hbm.at[:, :, lo:hi], basis_sem.at[t]))
        stores[-1].start()
    for store in stores:
        store.wait()


def factor(gram, matrix, scale, rows, cols):
    size, n = matrix.shape
    square = jax.ShapeDtypeStruct((n, n), jnp.float32)
    vmem = pl.BlockSpec(memory_space=pltpu.VMEM)
    return pl.pallas_call(
        functools.partial(factor_kernel, scale, n),
        out_shape=(square, jax.ShapeDtypeStruct((rows, cols, n), jnp.float32)),
        in_specs=[vmem, pl.BlockSpec(memory_space=pl.ANY)],
        out_specs=(pl.BlockSpec(memory_space=pl.ANY),) * 2,
        scratch_shapes=[
            pltpu.VMEM((size, n), jnp.float32), pltpu.VMEM((n, n), jnp.float32), pltpu.VMEM((rows, cols, n), jnp.float32),
            pltpu.VMEM((n, n), jnp.float32), pltpu.VMEM((LANES, LANES), jnp.float32),
            pltpu.VMEM((n, LANES), jnp.float32), pltpu.VMEM((size, n), jnp.float32),
            pltpu.SemaphoreType.DMA, pltpu.SemaphoreType.DMA((n // LANES,)), pltpu.SemaphoreType.DMA((n // LANES,)),
        ],
        name="factor",
    )(pltpu.with_memory_space_constraint(gram, pltpu.VMEM), matrix)


def front_kernel(n_lat, n_lon, pair, cols, group, x_ref, v_ref, lat_ref, lon_ref, w_ref, m_hbm, out_ref, m_ref, m_sem, flat, row_ref, band_ref, ext, lonb, g_ref, rbuf, zbuf, psend, precv, fsend, frecv, lsend, lrecv, ssem, rsem, zssem, zrsem, cssem, crsem):
    lat, lon = lax.axis_index("lat"), lax.axis_index("lon")
    n_p, n_z = n_lat * pair, n_lon // pair
    share = g_ref.shape[0] // n_p
    core, z = lax.rem(lon, pair), lon // pair
    me = lat * pair + core
    chunks, size = lonb.shape[0], lonb.shape[2]
    rows_lat = size // cols
    taps = lat_ref.shape[0]
    step = group * cols
    pieces = size // step
    odd = lax.rem(lat, 2)
    partner = lat + 1 - 2 * odd
    target = lat + 2 - 4 * odd
    source = lat - 2 + 4 * odd
    hands_on = jnp.logical_and(target >= 0, target < n_lat)
    gets = jnp.logical_and(source >= 0, source < n_lat)
    right, left = lax.rem(lon + 1, n_lon), lax.rem(lon + n_lon - 1, n_lon)
    far = 2 * size * odd
    near = 2 * size * (1 - odd)

    def plane_peer(o):
        peer = lax.rem(me + o, n_p)
        return peer, (peer // pair, z * pair + lax.rem(peer, pair))

    def z_peer(o):
        return (lat, lax.rem(z + o, n_z) * pair + core)

    barrier = pltpu.get_barrier_semaphore()
    for o in range(1, n_p):
        pl.semaphore_signal(barrier, inc=1, device_id=plane_peer(o)[1], device_id_type=MESH)
    for o in range(1, n_z):
        pl.semaphore_signal(barrier, inc=1, device_id=z_peer(o), device_id_type=MESH)
    for side_dev in (left, right):
        pl.semaphore_signal(barrier, inc=1, device_id=(lat, side_dev), device_id_type=MESH)

    def up(k):
        return k * step + odd * ((pieces - 1 - 2 * k) * step)

    def down(k):
        return (pieces - 1 - k) * step + odd * ((2 * k - pieces + 1) * step)

    def at(start):
        return pl.ds(pl.multiple_of(start, 8), step)

    def swap(c, k):
        return pltpu.make_async_remote_copy(
            src_ref=ext.at[c, at(size + up(k))], dst_ref=ext.at[c, at(far + up(k))],
            send_sem=psend.at[c, k], recv_sem=precv.at[c, k], device_id=(partner, lon), device_id_type=MESH)

    def hand(c, k):
        return pltpu.make_async_remote_copy(
            src_ref=ext.at[c, at(near + down(k))], dst_ref=ext.at[c, at(far + down(k))],
            send_sem=fsend.at[c, k], recv_sem=frecv.at[c, k], device_id=(target, lon), device_id_type=MESH)

    def side(c, k, way):
        start = up(k) if c else down(k)
        return pltpu.make_async_remote_copy(
            src_ref=lonb.at[c, 1, at(start)], dst_ref=lonb.at[c, 2 * way, at(start)],
            send_sem=lsend.at[c, k, way], recv_sem=lrecv.at[c, k, way],
            device_id=(lat, left if way else right), device_id_type=MESH)

    def relay(c, k):
        swap(c, k).wait_recv()

        @pl.when(hands_on)
        def _():
            hand(c, k).start()

    def lat_smooth(c, start):
        sums = {}
        for k in range(taps):
            place = (k + rows_lat - taps // 2) * cols
            q = place % 8
            rows = step + 8 if q else step
            value = lat_ref[k] * ext[c, pl.ds(pl.multiple_of(start + place - q, 8), rows)]
            sums[q] = sums[q] + value if q in sums else value
        return sum(v[q:q + step] for q, v in sums.items())

    def lon_smooth(c, start):
        value = jnp.concatenate([lonb[c, p, at(start)] for p in range(3)], axis=0)
        return jnp.dot(band_ref[...], value, precision=lax.Precision.HIGHEST, preferred_element_type=jnp.float32)

    def weighted(value, start):
        row = lat * rows_lat + start // cols
        place = lax.broadcasted_iota(jnp.int32, value.shape, 0)
        weight = jnp.zeros(value.shape, jnp.float32) + w_ref[row]
        for q in range(1, group):
            weight = jnp.where(place >= q * cols, w_ref[row + q], weight)
        return value * weight

    length = x_ref.shape[2]
    half = v_ref.shape[0]
    for i in range(rows_lat):
        flat[i * cols:(i + 1) * cols] = x_ref[i]
    span = row_ref.shape[1]
    lane = lax.broadcasted_iota(jnp.int32, (1, span), 1)
    row_ref[...] = jnp.zeros((1, span), jnp.float32)
    row_ref[:, :half] = v_ref[...].reshape(1, half)
    row = jnp.where(lane == half // 2, row_ref[...] + 1.0, row_ref[...])
    shifts = pltpu.roll(jnp.broadcast_to(row, (LANES, span)), 0, 1, stride=1, stride_axis=0)

    def filtered(c):
        return lax.dot_general(
            flat[:, c * LANES:c * LANES + span], shifts, (((1,), (1,)), ((), ())),
            precision=lax.Precision.HIGHEST, preferred_element_type=jnp.float32)

    ext[0, size:2 * size] = filtered(0)
    pl.semaphore_wait(barrier, n_p + n_z)
    for k in range(pieces):
        swap(0, k).start()
    lonb[1, 1] = filtered(1)
    for k in range(pieces):
        side(1, k, 0).start()
        side(1, k, 1).start()

    @pl.when(jnp.logical_not(gets))
    def _():
        for c in range(chunks):
            ext[c, pl.ds(pl.multiple_of(far, 8), size)] = jnp.zeros((size, LANES), jnp.float32)

    bands = 3
    shape = (step, bands * step)
    r, e = lax.broadcasted_iota(jnp.int32, shape, 0), lax.broadcasted_iota(jnp.int32, shape, 1)
    part = sum((e >= p * step).astype(jnp.int32) for p in range(1, bands)) + jnp.zeros(shape, jnp.int32)
    e = e - part * step
    er = sum((e >= q * cols).astype(jnp.int32) for q in range(1, group)) + jnp.zeros(shape, jnp.int32)
    rr = sum((r >= q * cols).astype(jnp.int32) for q in range(1, group)) + jnp.zeros(shape, jnp.int32)
    offset = part * cols + (e - er * cols) - (r - rr * cols) - (cols - taps // 2)
    offset = jnp.where(er == rr, offset, -1)
    band = jnp.zeros(shape, jnp.float32)
    for k in range(taps):
        band = jnp.where(offset == k, lon_ref[k], band)
    band_ref[...] = band

    def lon_first(k):
        side(1, k, 0).wait_recv()
        side(1, k, 1).wait_recv()
        ext[1, at(size + up(k))] = lon_smooth(1, up(k))
        swap(1, k).start()

    def lat_first(k):
        @pl.when(gets)
        def _():
            hand(0, k).wait_recv()

        lonb[0, 1, at(down(k))] = lat_smooth(0, down(k))
        side(0, k, 0).start()
        side(0, k, 1).start()

    def lon_last(k):
        side(0, k, 0).wait_recv()
        side(0, k, 1).wait_recv()
        m_ref[at(down(k)), :LANES] = weighted(lon_smooth(0, down(k)), down(k))

    def lat_last(k):
        @pl.when(gets)
        def _():
            hand(1, k).wait_recv()

        m_ref[at(down(k)), LANES:] = weighted(lat_smooth(1, down(k)), down(k))

    relay_0, relay_1 = functools.partial(relay, 0), functools.partial(relay, 1)
    order = [(k, relay_0, k) for k in range(pieces)]
    order += [(k + 1.5, lon_first, k) for k in range(pieces)]
    order += [(pieces - 0.8 + k, lat_first, k) for k in range(pieces)]
    order += [(pieces + 2.5 + k, relay_1, k) for k in range(pieces)]
    order += [(3 * pieces + k, lon_last, k) for k in range(pieces)]
    order += [(3 * pieces + k + 0.5, lat_last, k) for k in range(pieces)]
    for _, do, k in sorted(order, key=lambda item: item[0]):
        do(k)

    def mine(part, who):
        base, _, rows = part
        return pl.ds(pl.multiple_of(base + who * rows, 8), rows)

    def held(part):
        return pl.ds(part[1], part[2])

    def scatter(j):
        copies = []
        for o in range(1, n_p):
            peer, dev = plane_peer(o)
            c = pltpu.make_async_remote_copy(
                src_ref=g_ref.at[mine(parts[j], peer)], dst_ref=rbuf.at[o, held(parts[j])],
                send_sem=ssem.at[j, o], recv_sem=rsem.at[j, o], device_id=dev, device_id_type=MESH)
            c.start()
            copies.append(c)
        return copies

    keep = pltpu.make_async_copy(m_ref, m_hbm, m_sem)
    keep.start()
    parts = split_rows(share, n_p)
    sent = []
    place = 0
    tails = []
    for t in range(chunks):
        both = lax.dot_general(
            m_ref[:, t * LANES:(t + 1) * LANES], m_ref[:, t * LANES:], (((0,), (0,)), ((), ())),
            precision=lax.Precision.HIGHEST, preferred_element_type=jnp.float32)
        for r in range(2):
            for q in range(r, chunks - t):
                g_ref[place:place + HALF] = both[r * HALF:(r + 1) * HALF, q * LANES:(q + 1) * LANES]
                place += HALF
        tails.append(both[HALF:, :LANES])
        if len(tails) == 2 or t == chunks - 1:
            g_ref[place:place + HALF] = merge(tails[0], tails[-1])
            place += HALF
            tails = []
        if t == chunks - 1 and place < g_ref.shape[0]:
            g_ref[place:] = jnp.zeros((g_ref.shape[0] - place, LANES), jnp.float32)
            place = g_ref.shape[0]
        while len(sent) < len(parts) and parts[len(sent)][0] + n_p * parts[len(sent)][2] <= place:
            sent.append(scatter(len(sent)))

    for c in range(chunks):
        for k in range(pieces):
            swap(c, k).wait_send()
            side(c, k, 0).wait_send()
            side(c, k, 1).wait_send()

    @pl.when(hands_on)
    def _():
        for c in range(chunks):
            for k in range(pieces):
                hand(c, k).wait_send()

    along, back = [], []
    for j, part in enumerate(parts):
        acc = g_ref[mine(part, me), :]
        for o in range(1, n_p):
            sent[j][o - 1].wait_recv()
            acc = acc + rbuf[o, held(part)]
        zbuf[z, held(part)] = acc
        copies = []
        for o in range(1, n_z):
            c = pltpu.make_async_remote_copy(
                src_ref=zbuf.at[z, held(part)], dst_ref=zbuf.at[z, held(part)],
                send_sem=zssem.at[j, o], recv_sem=zrsem.at[j, o], device_id=z_peer(o), device_id_type=MESH)
            c.start()
            copies.append(c)
        along.append(copies)
    for j, part in enumerate(parts):
        for c in along[j]:
            c.wait_recv()
        total = zbuf[0, held(part)]
        for k in range(1, n_z):
            total = total + zbuf[k, held(part)]
        out_ref[mine(part, me), :] = total
        copies = []
        for o in range(1, n_p):
            c = pltpu.make_async_remote_copy(
                src_ref=out_ref.at[mine(part, me)], dst_ref=out_ref.at[mine(part, me)],
                send_sem=cssem.at[j, o], recv_sem=crsem.at[j, o], device_id=plane_peer(o)[1], device_id_type=MESH)
            c.start()
            copies.append(c)
        back.append(copies)
    for copies in sent + along:
        for c in copies:
            c.wait_send()
    keep.wait()
    for copies in back:
        for c in copies:
            c.wait()


def split_rows(share, n_p):
    first = share
    parts, base, off = [], 0, 0
    for rows in (first, share - first):
        if rows:
            parts.append((base, off, rows))
            base += n_p * rows
            off += rows
    return parts


def merge(left, right):
    lane = lax.broadcasted_iota(jnp.int32, left.shape, 1)
    return jnp.where(lane < HALF, pltpu.roll(left, HALF, 1), right)


def matrix_and_gram(field, time_taps, lat_kernel, lon_kernel, weights):
    rows_lat, cols, length = field.shape
    size = rows_lat * cols
    steps = length - time_taps.shape[0] + 1
    chunks = steps // LANES
    fits = [q for q in range(1, rows_lat + 1) if rows_lat % q == 0 and q * cols % 8 == 0]
    group = next((q for q in fits if q * cols >= 64), fits[-1])
    step = group * cols
    pieces = rows_lat // group
    span = -(-(LANES + time_taps.shape[0] - 1) // LANES) * LANES
    blocks = chunks * chunks + -(-chunks // 2)
    n_lat, n_lon = lax.axis_size("lat"), lax.axis_size("lon")
    pair = 2 if n_lon % 2 == 0 else 1
    n_p, n_z = n_lat * pair, n_lon // pair
    share = -(-(blocks * HALF) // (8 * n_p)) * 8
    packed = share * n_p
    parts = len(split_rows(share, n_p))
    dma = pltpu.SemaphoreType.DMA
    vmem, smem = pl.BlockSpec(memory_space=pltpu.VMEM), pl.BlockSpec(memory_space=pltpu.SMEM)
    return pl.pallas_call(
        functools.partial(front_kernel, n_lat, n_lon, pair, cols, group),
        out_shape=(jax.ShapeDtypeStruct((size, steps), jnp.float32), pltpu.VMEM((packed, LANES), jnp.float32)),
        in_specs=[vmem, vmem, smem, smem, smem],
        out_specs=(pl.BlockSpec(memory_space=pl.ANY), vmem),
        scratch_shapes=[
            pltpu.VMEM((size, steps), jnp.float32),
            dma,
            pltpu.VMEM((size, length), jnp.float32),
            pltpu.VMEM((1, span), jnp.float32),
            pltpu.VMEM((step, 3 * step), jnp.float32),
            pltpu.VMEM((chunks, 3 * size, LANES), jnp.float32),
            pltpu.VMEM((chunks, 3, size, LANES), jnp.float32),
            pltpu.VMEM((packed, LANES), jnp.float32),
            pltpu.VMEM((n_p, share, LANES), jnp.float32),
            pltpu.VMEM((n_z, share, LANES), jnp.float32),
        ] + [dma((chunks, pieces))] * 4 + [dma((chunks, pieces, 2))] * 2
        + [dma((parts, n_p))] * 2 + [dma((parts, n_z))] * 2 + [dma((parts, n_p))] * 2,
        compiler_params=pltpu.CompilerParams(collective_id=0, has_side_effects=True),
        name="front",
    )(field, time_taps, lat_kernel, lon_kernel, weights)


def body(field, lat_kernel, lon_kernel, time_taps):
    rows_lat, rows_lon = field.shape[:2]
    total_lat = rows_lat * lax.axis_size("lat")
    cells = total_lat * rows_lon * lax.axis_size("lon")
    latitude = np.pi * (np.arange(total_lat) + 0.5) / total_lat - np.pi / 2
    weights = jnp.asarray(np.sqrt(np.cos(latitude)), jnp.float32)
    matrix, gram = matrix_and_gram(field, time_taps, lat_kernel, lon_kernel, weights)
    upper, basis = factor(gram, matrix, float(cells) ** 0.5, rows_lat, rows_lon)
    return (basis, upper)


def solution(mesh):
    placed = (P("lat", "lon", None), P(), P(), P())
    return jax.shard_map(
        body, mesh=mesh, in_specs=placed, out_specs=(P("lat", "lon", None), P()), check_vma=False
    )
```

```python
import functools

import jax
import jax.numpy as jnp
import numpy as np
from jax import lax
from jax.experimental import pallas as pl
from jax.experimental.pallas import tpu as pltpu
from jax.sharding import PartitionSpec as P


MESH = pl.DeviceIdType.MESH
NB = 64
LANES = 128
HALF = LANES // 2


def spread(x, q):
    return jnp.broadcast_to(x[q:q + 1, :], (8, LANES))


def column(x, lane):
    return jnp.take_along_axis(x, jnp.full(x.shape, lane, jnp.int32), axis=1, mode="promise_in_bounds")


def eliminate(grp, first):
    sub = lax.broadcasted_iota(jnp.int32, (8, LANES), 0)
    tiles = range(len(grp[0]))
    for g in range(len(grp)):
        lane = first + 8 * g
        cols = [{h: column(grp[h][0], lane + q) for h in range(g, len(grp))} for q in range(8)]
        s = {(i, j): spread(cols[j][g], i) for j in range(8) for i in range(j, 8)}
        rows = [[spread(grp[g][t], q) for t in tiles] for q in range(8)]
        inv, low, pivots = [None] * 8, {}, None
        for q in range(8):
            if q % 2 == 0:
                inv[q] = pltpu.reciprocal(s[q, q])
                inv[q + 1] = s[q, q] * pltpu.reciprocal(s[q, q] * s[q + 1, q + 1] - s[q + 1, q] * s[q + 1, q])
            pivots = s[q, q] if pivots is None else jnp.where(sub == q, s[q, q], pivots)
            for i in range(q + 1, 8):
                low[i, q] = s[i, q] * inv[q]
            for j in range(q + 1, 8):
                for i in range(j, 8):
                    s[i, j] = s[i, j] - low[i, q] * s[j, q]
        for q in range(8):
            for p in range(q + 1, 8):
                for t in tiles:
                    rows[p][t] = rows[p][t] - low[p, q] * rows[q][t]
        for h in range(g + 1, len(grp)):
            for q in range(8):
                u = cols[q][h] * inv[q]
                for p in range(q + 1, 8):
                    cols[p][h] = cols[p][h] - u * s[p, q]
                for t in tiles:
                    grp[h][t] = grp[h][t] - u * rows[q][t]
        rinv = lax.rsqrt(pivots)
        for t in tiles:
            done = rows[0][t]
            for q in range(1, 8):
                done = jnp.where(sub == q, rows[q][t], done)
            grp[g][t] = done * rinv


def factor_kernel(scale, n, g_ref, m_ref, r_hbm, basis_hbm, r_ref, basis_ref, a, b, y_ref, p_ref, r_sem, basis_sem):
    stores = []
    at = 0
    first = column(spread(g_ref[0:8], 0), 0)[0:1, :]
    unit = 1.0 / first
    tiles = n // LANES
    tails = []
    for t in range(tiles):
        if t:
            a[t * LANES:(t + 1) * LANES, :t * LANES] = jnp.zeros((LANES, t * LANES), jnp.float32)
        for r in range(2):
            row = t * LANES + r * HALF
            for q in range(t + r, tiles):
                a[row:row + HALF, q * LANES:(q + 1) * LANES] = g_ref[at:at + HALF] * unit
                at += HALF
        tails.append(t)
        if len(tails) == 2 or t == tiles - 1:
            both = g_ref[at:at + HALF] * unit
            at += HALF
            lane = lax.broadcasted_iota(jnp.int32, both.shape, 1)
            for u in tails:
                tail = both if u % 2 or len(tails) == 1 else pltpu.roll(both, HALF, 1)
                a[u * LANES + HALF:(u + 1) * LANES, u * LANES:(u + 1) * LANES] = jnp.where(lane < HALF, 0.0, tail)
            tails = []
    root = lax.sqrt(first)[:, :1]
    to_r = root / scale
    to_y = scale / root
    rows, cols = basis_hbm.shape[:2]
    down = (((0,), (0,)), ((), ()))
    flat = (((1,), (0,)), ((), ()))
    across = (((1,), (1,)), ((), ()))

    def dot(x, y, dims):
        return lax.dot_general(x, y, dims, precision=lax.Precision.HIGHEST, preferred_element_type=jnp.float32)

    square = (LANES, LANES)
    eye = (lax.broadcasted_iota(jnp.int32, square, 0) == lax.broadcasted_iota(jnp.int32, square, 1)).astype(jnp.float32)
    for t in range(tiles):
        lo, hi = t * LANES, (t + 1) * LANES
        wide = n - lo
        b[...] = eye
        for k in range(lo, hi, NB):
            live = [(a, k, q) for q in range(t, tiles)] + [(b, k - lo, 0)]
            grp = [[ref[r + 8 * h:r + 8 * h + 8, q * LANES:(q + 1) * LANES] for ref, r, q in live] for h in range(NB // 8)]
            eliminate(grp, k - lo)
            panel = jnp.concatenate([jnp.concatenate(x, axis=1) for x in grp], axis=0)
            nxt = k + NB
            if nxt < hi:
                update = dot(panel[:, nxt - lo:LANES], panel, down)
                a[nxt:hi, lo:] = a[nxt:hi, lo:] - update[:, :wide]
                b[nxt - lo:, :] = b[nxt - lo:, :] - update[:, wide:]
            row_id = lax.broadcasted_iota(jnp.int32, (NB, wide), 0) + k
            lane_id = lax.broadcasted_iota(jnp.int32, (NB, wide), 1) + lo
            if t:
                r_ref[k:nxt, :lo] = jnp.zeros((NB, lo), jnp.float32)
            r_ref[k:nxt, lo:] = jnp.where(lane_id >= row_id, panel[:, :wide] * to_r, 0.0)
            y_ref[k:nxt, :] = panel[:, wide:]
            if hi < n:
                a[k:nxt, hi:] = panel[:, LANES:wide]
        if hi < n:
            a[hi:, hi:] = a[hi:, hi:] - dot(a[lo:hi, hi:], a[lo:hi, hi:], down)
        stores.append(pltpu.make_async_copy(r_ref.at[lo:hi], r_hbm.at[lo:hi], r_sem.at[t]))
        stores[-1].start()
        part = dot(p_ref[:, lo:hi] if t else m_ref[:, lo:hi], y_ref[lo:hi, :], across)
        if hi < n:
            p_ref[:, hi:] = (p_ref[:, hi:] if t else m_ref[:, hi:]) - dot(part, a[lo:hi, hi:], flat)
        for i in range(rows):
            basis_ref[i, :, lo:hi] = part[i * cols:(i + 1) * cols] * to_y
        stores.append(pltpu.make_async_copy(basis_ref.at[:, :, lo:hi], basis_hbm.at[:, :, lo:hi], basis_sem.at[t]))
        stores[-1].start()
    for store in stores:
        store.wait()


def factor(gram, matrix, scale, rows, cols):
    size, n = matrix.shape
    square = jax.ShapeDtypeStruct((n, n), jnp.float32)
    vmem = pl.BlockSpec(memory_space=pltpu.VMEM)
    return pl.pallas_call(
        functools.partial(factor_kernel, scale, n),
        out_shape=(square, jax.ShapeDtypeStruct((rows, cols, n), jnp.float32)),
        in_specs=[vmem, vmem],
        out_specs=(pl.BlockSpec(memory_space=pl.ANY),) * 2,
        scratch_shapes=[
            pltpu.VMEM((n, n), jnp.float32), pltpu.VMEM((rows, cols, n), jnp.float32),
            pltpu.VMEM((n, n), jnp.float32), pltpu.VMEM((LANES, LANES), jnp.float32),
            pltpu.VMEM((n, LANES), jnp.float32), pltpu.VMEM((size, n), jnp.float32),
            pltpu.SemaphoreType.DMA((n // LANES,)), pltpu.SemaphoreType.DMA((n // LANES,)),
        ],
        name="factor",
    )(*(pltpu.with_memory_space_constraint(x, pltpu.VMEM) for x in (gram, matrix)))


def front_kernel(n_lat, n_lon, pair, cols, group, x_hbm, v_ref, lat_ref, lon_ref, w_ref, m_ref, out_ref, x_ref, x_sem, flat, row_ref, band_ref, ext, lonb, g_ref, rbuf, zbuf, psend, precv, fsend, frecv, lsend, lrecv, ssem, rsem, zssem, zrsem, cssem, crsem):
    load = pltpu.make_async_copy(x_hbm, x_ref, x_sem)
    load.start()
    lat, lon = lax.axis_index("lat"), lax.axis_index("lon")
    n_p, n_z = n_lat * pair, n_lon // pair
    share = g_ref.shape[0] // n_p
    core, z = lax.rem(lon, pair), lon // pair
    me = lat * pair + core
    chunks, size = lonb.shape[0], lonb.shape[2]
    rows_lat = size // cols
    taps = lat_ref.shape[0]
    step = group * cols
    pieces = size // step
    odd = lax.rem(lat, 2)
    partner = lat + 1 - 2 * odd
    target = lat + 2 - 4 * odd
    source = lat - 2 + 4 * odd
    hands_on = jnp.logical_and(target >= 0, target < n_lat)
    gets = jnp.logical_and(source >= 0, source < n_lat)
    right, left = lax.rem(lon + 1, n_lon), lax.rem(lon + n_lon - 1, n_lon)
    far = 2 * size * odd
    near = 2 * size * (1 - odd)

    def plane_peer(o):
        peer = lax.rem(me + o, n_p)
        return peer, (peer // pair, z * pair + lax.rem(peer, pair))

    def z_peer(o):
        return (lat, lax.rem(z + o, n_z) * pair + core)

    barrier = pltpu.get_barrier_semaphore()
    for o in range(1, n_p):
        pl.semaphore_signal(barrier, inc=1, device_id=plane_peer(o)[1], device_id_type=MESH)
    for o in range(1, n_z):
        pl.semaphore_signal(barrier, inc=1, device_id=z_peer(o), device_id_type=MESH)
    for side_dev in (left, right):
        pl.semaphore_signal(barrier, inc=1, device_id=(lat, side_dev), device_id_type=MESH)

    def up(k):
        return k * step + odd * ((pieces - 1 - 2 * k) * step)

    def down(k):
        return (pieces - 1 - k) * step + odd * ((2 * k - pieces + 1) * step)

    def at(start):
        return pl.ds(pl.multiple_of(start, 8), step)

    def swap(c, k):
        return pltpu.make_async_remote_copy(
            src_ref=ext.at[c, at(size + up(k))], dst_ref=ext.at[c, at(far + up(k))],
            send_sem=psend.at[c, k], recv_sem=precv.at[c, k], device_id=(partner, lon), device_id_type=MESH)

    def hand(c, k):
        return pltpu.make_async_remote_copy(
            src_ref=ext.at[c, at(near + down(k))], dst_ref=ext.at[c, at(far + down(k))],
            send_sem=fsend.at[c, k], recv_sem=frecv.at[c, k], device_id=(target, lon), device_id_type=MESH)

    def side(c, k, way):
        start = up(k) if c else down(k)
        return pltpu.make_async_remote_copy(
            src_ref=lonb.at[c, 1, at(start)], dst_ref=lonb.at[c, 2 * way, at(start)],
            send_sem=lsend.at[c, k, way], recv_sem=lrecv.at[c, k, way],
            device_id=(lat, left if way else right), device_id_type=MESH)

    def relay(c, k):
        swap(c, k).wait_recv()

        @pl.when(hands_on)
        def _():
            hand(c, k).start()

    def lat_smooth(c, start):
        sums = {}
        for k in range(taps):
            place = (k + rows_lat - taps // 2) * cols
            q = place % 8
            rows = step + 8 if q else step
            value = lat_ref[k] * ext[c, pl.ds(pl.multiple_of(start + place - q, 8), rows)]
            sums[q] = sums[q] + value if q in sums else value
        return sum(v[q:q + step] for q, v in sums.items())

    def lon_smooth(c, start):
        value = jnp.concatenate([lonb[c, p, at(start)] for p in range(3)], axis=0)
        return jnp.dot(band_ref[...], value, precision=lax.Precision.HIGHEST, preferred_element_type=jnp.float32)

    def weighted(value, start):
        row = lat * rows_lat + start // cols
        place = lax.broadcasted_iota(jnp.int32, value.shape, 0)
        weight = jnp.zeros(value.shape, jnp.float32) + w_ref[row]
        for q in range(1, group):
            weight = jnp.where(place >= q * cols, w_ref[row + q], weight)
        return value * weight

    length = x_ref.shape[2]
    half = v_ref.shape[0]
    span = row_ref.shape[1]
    lane = lax.broadcasted_iota(jnp.int32, (1, span), 1)
    row_ref[...] = jnp.zeros((1, span), jnp.float32)
    row_ref[:, :half] = v_ref[...].reshape(1, half)
    row = jnp.where(lane == half // 2, row_ref[...] + 1.0, row_ref[...])
    shifts = pltpu.roll(jnp.broadcast_to(row, (LANES, span)), 0, 1, stride=1, stride_axis=0)

    load.wait()
    for i in range(rows_lat):
        flat[i * cols:(i + 1) * cols] = x_ref[i]

    def filtered(c):
        return lax.dot_general(
            flat[:, c * LANES:c * LANES + span], shifts, (((1,), (1,)), ((), ())),
            precision=lax.Precision.HIGHEST, preferred_element_type=jnp.float32)

    ext[0, size:2 * size] = filtered(0)
    pl.semaphore_wait(barrier, n_p + n_z)
    for k in range(pieces):
        swap(0, k).start()
    lonb[1, 1] = filtered(1)
    for k in range(pieces):
        side(1, k, 0).start()
        side(1, k, 1).start()

    @pl.when(jnp.logical_not(gets))
    def _():
        for c in range(chunks):
            ext[c, pl.ds(pl.multiple_of(far, 8), size)] = jnp.zeros((size, LANES), jnp.float32)

    bands = 3
    shape = (step, bands * step)
    r, e = lax.broadcasted_iota(jnp.int32, shape, 0), lax.broadcasted_iota(jnp.int32, shape, 1)
    part = sum((e >= p * step).astype(jnp.int32) for p in range(1, bands)) + jnp.zeros(shape, jnp.int32)
    e = e - part * step
    er = sum((e >= q * cols).astype(jnp.int32) for q in range(1, group)) + jnp.zeros(shape, jnp.int32)
    rr = sum((r >= q * cols).astype(jnp.int32) for q in range(1, group)) + jnp.zeros(shape, jnp.int32)
    offset = part * cols + (e - er * cols) - (r - rr * cols) - (cols - taps // 2)
    offset = jnp.where(er == rr, offset, -1)
    band = jnp.zeros(shape, jnp.float32)
    for k in range(taps):
        band = jnp.where(offset == k, lon_ref[k], band)
    band_ref[...] = band

    def lon_first(k):
        side(1, k, 0).wait_recv()
        side(1, k, 1).wait_recv()
        ext[1, at(size + up(k))] = lon_smooth(1, up(k))
        swap(1, k).start()

    def lat_first(k):
        @pl.when(gets)
        def _():
            hand(0, k).wait_recv()

        lonb[0, 1, at(down(k))] = lat_smooth(0, down(k))
        side(0, k, 0).start()
        side(0, k, 1).start()

    def lon_last(k):
        side(0, k, 0).wait_recv()
        side(0, k, 1).wait_recv()
        m_ref[at(down(k)), :LANES] = weighted(lon_smooth(0, down(k)), down(k))

    def lat_last(k):
        @pl.when(gets)
        def _():
            hand(1, k).wait_recv()

        m_ref[at(down(k)), LANES:] = weighted(lat_smooth(1, down(k)), down(k))

    relay_0, relay_1 = functools.partial(relay, 0), functools.partial(relay, 1)
    order = [(k, relay_0, k) for k in range(pieces)]
    order += [(k + 1.5, lon_first, k) for k in range(pieces)]
    order += [(pieces - 0.8 + k, lat_first, k) for k in range(pieces)]
    order += [(pieces + 2.5 + k, relay_1, k) for k in range(pieces)]
    order += [(3 * pieces + k, lon_last, k) for k in range(pieces)]
    order += [(3 * pieces + k + 0.5, lat_last, k) for k in range(pieces)]
    for _, do, k in sorted(order, key=lambda item: item[0]):
        do(k)

    def mine(part, who):
        base, _, rows = part
        return pl.ds(pl.multiple_of(base + who * rows, 8), rows)

    def held(part):
        return pl.ds(part[1], part[2])

    def scatter(j):
        copies = []
        for o in range(1, n_p):
            peer, dev = plane_peer(o)
            c = pltpu.make_async_remote_copy(
                src_ref=g_ref.at[mine(parts[j], peer)], dst_ref=rbuf.at[o, held(parts[j])],
                send_sem=ssem.at[j, o], recv_sem=rsem.at[j, o], device_id=dev, device_id_type=MESH)
            c.start()
            copies.append(c)
        return copies

    parts = split_rows(share, n_p)
    sent = []
    place = 0
    tails = []
    for t in range(chunks):
        both = lax.dot_general(
            m_ref[:, t * LANES:(t + 1) * LANES], m_ref[:, t * LANES:], (((0,), (0,)), ((), ())),
            precision=lax.Precision.HIGHEST, preferred_element_type=jnp.float32)
        for r in range(2):
            for q in range(r, chunks - t):
                g_ref[place:place + HALF] = both[r * HALF:(r + 1) * HALF, q * LANES:(q + 1) * LANES]
                place += HALF
        tails.append(both[HALF:, :LANES])
        if len(tails) == 2 or t == chunks - 1:
            g_ref[place:place + HALF] = merge(tails[0], tails[-1])
            place += HALF
            tails = []
        if t == chunks - 1 and place < g_ref.shape[0]:
            g_ref[place:] = jnp.zeros((g_ref.shape[0] - place, LANES), jnp.float32)
            place = g_ref.shape[0]
        while len(sent) < len(parts) and parts[len(sent)][0] + n_p * parts[len(sent)][2] <= place:
            sent.append(scatter(len(sent)))

    for c in range(chunks):
        for k in range(pieces):
            swap(c, k).wait_send()
            side(c, k, 0).wait_send()
            side(c, k, 1).wait_send()

    @pl.when(hands_on)
    def _():
        for c in range(chunks):
            for k in range(pieces):
                hand(c, k).wait_send()

    along, back = [], []
    for j, part in enumerate(parts):
        acc = g_ref[mine(part, me), :]
        for o in range(1, n_p):
            sent[j][o - 1].wait_recv()
            acc = acc + rbuf[o, held(part)]
        zbuf[z, held(part)] = acc
        copies = []
        for o in range(1, n_z):
            c = pltpu.make_async_remote_copy(
                src_ref=zbuf.at[z, held(part)], dst_ref=zbuf.at[z, held(part)],
                send_sem=zssem.at[j, o], recv_sem=zrsem.at[j, o], device_id=z_peer(o), device_id_type=MESH)
            c.start()
            copies.append(c)
        along.append(copies)
    for j, part in enumerate(parts):
        for c in along[j]:
            c.wait_recv()
        total = zbuf[0, held(part)]
        for k in range(1, n_z):
            total = total + zbuf[k, held(part)]
        out_ref[mine(part, me), :] = total
        copies = []
        for o in range(1, n_p):
            c = pltpu.make_async_remote_copy(
                src_ref=out_ref.at[mine(part, me)], dst_ref=out_ref.at[mine(part, me)],
                send_sem=cssem.at[j, o], recv_sem=crsem.at[j, o], device_id=plane_peer(o)[1], device_id_type=MESH)
            c.start()
            copies.append(c)
        back.append(copies)
    for copies in sent + along:
        for c in copies:
            c.wait_send()
    for copies in back:
        for c in copies:
            c.wait()


def split_rows(share, n_p):
    first = share
    parts, base, off = [], 0, 0
    for rows in (first, share - first):
        if rows:
            parts.append((base, off, rows))
            base += n_p * rows
            off += rows
    return parts


def merge(left, right):
    lane = lax.broadcasted_iota(jnp.int32, left.shape, 1)
    return jnp.where(lane < HALF, pltpu.roll(left, HALF, 1), right)


def matrix_and_gram(field, time_taps, lat_kernel, lon_kernel, weights):
    rows_lat, cols, length = field.shape
    size = rows_lat * cols
    steps = length - time_taps.shape[0] + 1
    chunks = steps // LANES
    fits = [q for q in range(1, rows_lat + 1) if rows_lat % q == 0 and q * cols % 8 == 0]
    group = next((q for q in fits if q * cols >= 64), fits[-1])
    step = group * cols
    pieces = rows_lat // group
    span = -(-(LANES + time_taps.shape[0] - 1) // LANES) * LANES
    blocks = chunks * chunks + -(-chunks // 2)
    n_lat, n_lon = lax.axis_size("lat"), lax.axis_size("lon")
    pair = 2 if n_lon % 2 == 0 else 1
    n_p, n_z = n_lat * pair, n_lon // pair
    share = -(-(blocks * HALF) // (8 * n_p)) * 8
    packed = share * n_p
    parts = len(split_rows(share, n_p))
    dma = pltpu.SemaphoreType.DMA
    vmem, smem = pl.BlockSpec(memory_space=pltpu.VMEM), pl.BlockSpec(memory_space=pltpu.SMEM)
    return pl.pallas_call(
        functools.partial(front_kernel, n_lat, n_lon, pair, cols, group),
        out_shape=(pltpu.VMEM((size, steps), jnp.float32), pltpu.VMEM((packed, LANES), jnp.float32)),
        in_specs=[pl.BlockSpec(memory_space=pl.ANY), vmem, smem, smem, smem],
        out_specs=(vmem, vmem),
        scratch_shapes=[
            pltpu.VMEM((rows_lat, cols, length), jnp.float32),
            dma,
            pltpu.VMEM((size, length), jnp.float32),
            pltpu.VMEM((1, span), jnp.float32),
            pltpu.VMEM((step, 3 * step), jnp.float32),
            pltpu.VMEM((chunks, 3 * size, LANES), jnp.float32),
            pltpu.VMEM((chunks, 3, size, LANES), jnp.float32),
            pltpu.VMEM((packed, LANES), jnp.float32),
            pltpu.VMEM((n_p, share, LANES), jnp.float32),
            pltpu.VMEM((n_z, share, LANES), jnp.float32),
        ] + [dma((chunks, pieces))] * 4 + [dma((chunks, pieces, 2))] * 2
        + [dma((parts, n_p))] * 2 + [dma((parts, n_z))] * 2 + [dma((parts, n_p))] * 2,
        compiler_params=pltpu.CompilerParams(collective_id=0, has_side_effects=True),
        name="front",
    )(field, time_taps, lat_kernel, lon_kernel, weights)


def body(field, lat_kernel, lon_kernel, time_taps):
    rows_lat, rows_lon = field.shape[:2]
    total_lat = rows_lat * lax.axis_size("lat")
    cells = total_lat * rows_lon * lax.axis_size("lon")
    latitude = np.pi * (np.arange(total_lat) + 0.5) / total_lat - np.pi / 2
    weights = jnp.asarray(np.sqrt(np.cos(latitude)), jnp.float32)
    matrix, gram = matrix_and_gram(field, time_taps, lat_kernel, lon_kernel, weights)
    upper, basis = factor(gram, matrix, float(cells) ** 0.5, rows_lat, rows_lon)
    return (basis, upper)


def solution(mesh):
    placed = (P("lat", "lon", None), P(), P(), P())
    return jax.shard_map(
        body, mesh=mesh, in_specs=placed, out_specs=(P("lat", "lon", None), P()), check_vma=False
    )
```
